32 devices in a mesh: ctx: 8 (over z, x), head: 2 (over y), dp: 2 (over core).
Axes of the slice: x: 2, y: 2, z: 4, core: 2. Of those that a mesh axis runs over, the one named last changes fastest.
Arguments:
- queries: bfloat16 [2, 2048, 32, 128], P('dp', 'ctx', 'head'), may hold values from -7 to 7
- keys: bfloat16 [2, 2048, 16, 128], P('dp', 'ctx', 'head'), may hold values from -7 to 7
- values: bfloat16 [2, 2048, 16, 128], P('dp', 'ctx', 'head'), may hold values from -6 to 6
- d_out: bfloat16 [2, 2048, 32, 128], P('dp', 'ctx', 'head'), may hold values from -6 to 6
- loss_mask: int32 [2, 2048], P('dp', 'ctx'), may hold values from 0 to 1, as said below
- turn_ids: int32 [2, 2048], P('dp', 'ctx'), may hold values from 0 to 1, never falling along the last dimension, each value on 1 to 1536 neighbouring positions
Outputs:
- d_queries: bfloat16 [2, 2048, 32, 128], P('dp', 'ctx', 'head')
- d_keys: bfloat16 [2, 2048, 16, 128], P('dp', 'ctx', 'head')
- d_values: bfloat16 [2, 2048, 16, 128], P('dp', 'ctx', 'head')
The draws below stay inside these ranges and needn't reach their ends.
Inputs may be any that keep to these rules, and one draw needn't show every extreme that they name: `loss_mask`: within each trajectory the share of ones grows with the position; position 0 of every trajectory is 1. `turn_ids`: turn ids never fall along a trajectory; each turn holds 1 to 1536 positions.
All inputs are finite; a program needn't handle non-finite values.
Results may differ from the reference program's by a relative error of at most 0.015.
Values may be sent and summed in bfloat16 or wider, within the bound.
A program may use at most 128 MiB of HBM per device.

```python
import math
import jax
import jax.numpy as jnp
import numpy as np
from jax import lax

QH = 32
KVH = 16
DH = 128
WINDOW = 1024
TOK_DEV = 256
TRAJ = 2
SEQ = 2048
TURNS = 2


def draw_loss_mask(key, part):
    span_count = SEQ // 8
    draw_values = jax.random.randint(jax.random.fold_in(key, 11), (TRAJ, span_count), 0, 5 * SEQ)
    span_start = jnp.arange(span_count, dtype=jnp.int32) * 8
    kept = (draw_values < SEQ + 3 * span_start[None, :]).astype(jnp.int32)
    mask_full = jnp.repeat(kept, 8, axis=1)
    return mask_full.at[:, 0].set(1)


def attention_pair(key):
    base_key = jax.random.fold_in(key, 23)
    subkeys = jax.random.split(base_key, 2)
    query_shape = (TRAJ, SEQ, QH, DH)
    key_shape = (TRAJ, SEQ, KVH, DH)
    query_new = jnp.clip(jax.random.normal(subkeys[0], query_shape, jnp.float32), -6.0, 6.0)
    key_new = jnp.clip(jax.random.normal(subkeys[1], key_shape, jnp.float32), -6.0, 6.0)
    return (query_new.astype(jnp.bfloat16), key_new.astype(jnp.bfloat16))


def draw_queries(key, part):
    return attention_pair(key)[0]


def draw_keys(key, part):
    return attention_pair(key)[1]


def block_scale(stream_key, shape, cuts, low, high):
    def one(axis_at, parts):
        heights = jax.random.uniform(jax.random.fold_in(jax.random.fold_in(stream_key, 6), axis_at), (parts,), jnp.float32, low / len(cuts), high / len(cuts))
        return jnp.repeat(jnp.exp(heights), shape[axis_at] // parts).reshape((-1,) + (1,) * (len(shape) - axis_at - 1))

    level = one(*cuts[0])
    for cut in cuts[1:]:
        level = level * one(*cut)
    return level


def profile(count, total, most, lean):
    loads = [(1 << 20) // math.isqrt(rank ** lean) + 1 for rank in range(2, count + 1)]
    spare, counts = total - most - (count - 1), [1] * (count - 1)
    while spare > 0:
        free = [i for i in range(count - 1) if counts[i] < most]
        whole, budget = sum([loads[i] for i in free]), spare
        for i in free:
            more = min(most - counts[i], max(1, budget * loads[i] // whole), spare)
            counts[i] = counts[i] + more
            spare = spare - more
    return np.array([most] + counts)


def ragged_sizes(stream_key, number_of, total, reach, lean):
    if number_of == 2:
        one = jax.random.randint(stream_key, (), max(1, total - reach), min(reach, total - 1) + 1)
        return jnp.stack([one, total - one])
    tallies = jnp.asarray(profile(number_of, total, reach, lean), jnp.int32)
    twos = (number_of - 1) // 2
    donor, taker = tallies[1:1 + 2 * twos:2], tallies[2:2 + 2 * twos:2]
    slack = jnp.minimum(donor - 1, reach - taker)
    passed = jax.random.randint(jax.random.fold_in(stream_key, 1), (twos,), 0, 1 << 20) % (slack + 1)
    tallies = tallies.at[1:1 + 2 * twos:2].set(donor - passed).at[2:2 + 2 * twos:2].set(taker + passed)
    return tallies[jax.random.permutation(jax.random.fold_in(stream_key, 2), number_of)]


def bell_draw(rng, shape, scale, bound, shards=(), kind=jnp.bfloat16):
    level = block_scale(rng, shape, shards, -0.22, 0.18) if shards else 1.0
    values = jax.random.normal(rng, shape, jnp.float32) * scale * level
    return jnp.minimum(jnp.maximum(values, -bound), bound).astype(kind)


def setup_inputs(seed: int = 0) -> dict:
    streams_of = jax.random.split(jax.random.key(seed), 7)
    return {
        "queries": draw_queries(jax.random.fold_in(streams_of[6], 71), 0),
        "keys": draw_keys(jax.random.fold_in(streams_of[6], 71), 0),
        "values": bell_draw(streams_of[2], (TRAJ, SEQ, KVH, DH), 1.0, 6.0, ((0, 2), (1, 8), (2, 2))),
        "d_out": bell_draw(streams_of[3], (TRAJ, SEQ, QH, DH), 1.0, 6.0, ((0, 2), (1, 8), (2, 2))),
        "loss_mask": draw_loss_mask(jax.random.fold_in(streams_of[6], 71), 0),
        "turn_ids": jax.vmap(lambda own: jnp.searchsorted(jnp.cumsum(ragged_sizes(own, TURNS, SEQ, 6 * TOK_DEV, 0)), jnp.arange(SEQ), side="right"))(jax.random.split(streams_of[5], TRAJ)).reshape((TRAJ, SEQ)).astype(jnp.int32),
    }


SCALE = 168.0 ** -0.5


def round_keep(array):
    return lax.optimization_barrier(array.astype(jnp.bfloat16)).astype(jnp.float32)


def reference(queries, keys, values, d_out, loss_mask, turn_ids):
    count_all = jnp.sum(loss_mask).astype(jnp.float32)
    factor = (TRAJ * SEQ) / count_all
    group_size = QH // KVH
    key_span = WINDOW + TOK_DEV
    row_index = lax.broadcasted_iota(jnp.int32, (TOK_DEV, key_span), 0)
    col_index = lax.broadcasted_iota(jnp.int32, (TOK_DEV, key_span), 1)
    query_list = []
    key_list = []
    value_list = []
    for member in range(TRAJ):
        query_all = queries[member].astype(jnp.float32).reshape(SEQ, KVH, group_size, DH)
        weighted = d_out[member] * loss_mask[member][:, None, None].astype(jnp.bfloat16)
        grad_all = weighted.astype(jnp.float32).reshape(SEQ, KVH, group_size, DH)
        pad_keys = jnp.concatenate([jnp.zeros((WINDOW, KVH, DH), jnp.float32), keys[member].astype(jnp.float32)], 0)
        pad_values = jnp.concatenate([jnp.zeros((WINDOW, KVH, DH), jnp.float32), values[member].astype(jnp.float32)], 0)
        turn_marks = (turn_ids[member] + 1).astype(jnp.int32)
        pad_marks = jnp.concatenate([jnp.zeros((WINDOW,), jnp.int32), turn_marks], 0)

        def block_step(running, block_index):
            key_acc, value_acc = running
            offset = (block_index * TOK_DEV).astype(jnp.int32)
            query_block = lax.dynamic_slice_in_dim(query_all, offset, TOK_DEV, 0)
            grad_block = lax.dynamic_slice_in_dim(grad_all, offset, TOK_DEV, 0)
            key_block = lax.dynamic_slice_in_dim(pad_keys, offset, key_span, 0)
            value_block = lax.dynamic_slice_in_dim(pad_values, offset, key_span, 0)
            mark_query = lax.dynamic_slice_in_dim(turn_marks, offset, TOK_DEV, 0)
            mark_key = lax.dynamic_slice_in_dim(pad_marks, offset, key_span, 0)
            allowed = (col_index > row_index) & (col_index <= row_index + WINDOW) & (mark_key[None, :] == mark_query[:, None])
            logits = jnp.einsum("tkgd,jkd->kgtj", query_block, key_block) * SCALE
            logits = jnp.where(allowed, logits, -jnp.inf)
            top_score = jnp.max(logits, axis=3, keepdims=True)
            raised = jnp.exp(logits - top_score)
            totals = jnp.sum(raised, axis=3, keepdims=True)
            prob_f32 = raised / totals
            prob_round = round_keep(prob_f32)
            outputs = round_keep(jnp.einsum("kgtj,jkd->tkgd", prob_round, value_block))
            deltas = jnp.sum(grad_block * outputs, axis=3)
            grad_probs = jnp.einsum("tkgd,jkd->kgtj", grad_block, value_block)
            grad_logits = prob_f32 * (grad_probs - jnp.transpose(deltas, (1, 2, 0))[..., None]) * SCALE
            grad_round = round_keep(grad_logits)
            grad_query = jnp.einsum("kgtj,jkd->tkgd", grad_round, key_block)
            grad_key = jnp.einsum("kgtj,tkgd->jkd", grad_round, query_block)
            grad_value = jnp.einsum("kgtj,tkgd->jkd", prob_round, grad_block)
            key_acc = lax.dynamic_update_slice_in_dim(key_acc, lax.dynamic_slice_in_dim(key_acc, offset, key_span, 0) + grad_key, offset, 0)
            value_acc = lax.dynamic_update_slice_in_dim(value_acc, lax.dynamic_slice_in_dim(value_acc, offset, key_span, 0) + grad_value, offset, 0)
            return (key_acc, value_acc), grad_query

        start_acc = jnp.zeros((WINDOW + SEQ, KVH, DH), jnp.float32)
        finals, grad_query = lax.scan(block_step, (start_acc, start_acc), jnp.arange(SEQ // TOK_DEV, dtype=jnp.int32))
        query_list.append((grad_query.reshape(SEQ, QH, DH) * factor).astype(jnp.bfloat16))
        key_list.append((finals[0][WINDOW:] * factor).astype(jnp.bfloat16))
        value_list.append((finals[1][WINDOW:] * factor).astype(jnp.bfloat16))
    return jnp.stack(query_list), jnp.stack(key_list), jnp.stack(value_list)
```

```python
import functools
import math

import jax
import jax.numpy as jnp
from jax import lax
from jax.experimental import pallas as pl
from jax.experimental.pallas import tpu as pltpu
from jax.sharding import PartitionSpec as P

WINDOW = 1024
SCALE = 168.0 ** (-0.5)
STRIP = 128
SPAN = WINDOW + STRIP
MASKED = -1e30


def strip_grads(c, strip, slot, qq, gg, ext, bias, acc, factor, dq_send):
    low = strip * STRIP
    query = qq[c, strip]
    grad = gg[c, strip]
    key = ext[c, 0, low : low + SPAN, :]
    value = ext[c, 1, low : low + SPAN, :]
    logits = lax.dot_general(
        key, query, (((1,), (1,)), ((), ())), preferred_element_type=jnp.float32
    )
    logits = logits * (SCALE * math.log2(math.e)) + bias[strip]
    top = jnp.max(logits, axis=0, keepdims=True)
    raised = jnp.exp2(logits - top)
    prob = raised * (1.0 / jnp.sum(raised, axis=0, keepdims=True))
    grad_prob = lax.dot_general(
        value, grad, (((1,), (1,)), ((), ())), preferred_element_type=jnp.float32
    )
    delta = jnp.sum(prob * grad_prob, axis=0, keepdims=True)
    grad_logit = (prob * (grad_prob - delta)).astype(jnp.bfloat16)
    dq = lax.dot_general(
        grad_logit, key, (((0,), (0,)), ((), ())), preferred_element_type=jnp.float32
    )
    dq_send[c, strip] = (dq * (factor * SCALE)).astype(jnp.bfloat16)
    parts = (
        jnp.dot(grad_logit, query, preferred_element_type=jnp.float32),
        jnp.dot(prob.astype(jnp.bfloat16), grad, preferred_element_type=jnp.float32),
    )
    for kind, part in enumerate(parts):
        if strip == 0:
            acc[slot, kind, :SPAN] = part
        else:
            acc[slot, kind, low : low + WINDOW] += part[:WINDOW]
            acc[slot, kind, low + WINDOW : low + SPAN] = part[WINDOW:]


def kernel(
    n, pairs, rows, q_ref, g_ref, kv_ref, turn_ref, mask_ref,
    dq_ref, dkv_ref,
    ext, qq, gg, acc, bias, column, dq_send, dkv_send, far, far_in, near, near_in,
    mark_ref, marks, count, count_in,
    mark_send, mark_recv, count_send, count_recv, local_sem,
    in_send, in_recv, far_send, far_recv, near_send, near_recv,
    dq_ssem, dq_rsem, dkv_ssem, dkv_rsem,
):
    heads = kv_ref.shape[0]
    half = heads // 2
    plane = 2 * rows
    planes = n // 2
    strips = plane // STRIP
    me = lax.axis_index("ctx")
    x = me % 2
    p = me // 2
    up, down = p + 1 < planes, p >= 1
    mine, theirs = x * half, (1 - x) * half
    bits = [("ctx", 1 << b) for b in range(n.bit_length() - 1)]
    bits += [("dp", 1 << b) for b in range(pairs.bit_length() - 1)]
    across, above, below = {"ctx": me + 1 - 2 * x}, {"ctx": me + 2}, {"ctx": me - 2}

    def remote(src, dst, send, recv, device):
        return pltpu.make_async_remote_copy(
            src_ref=src, dst_ref=dst, send_sem=send, recv_sem=recv,
            device_id=device, device_id_type=pl.DeviceIdType.MESH,
        )

    def partner(axis, bit):
        at = lax.axis_index(axis)
        return {axis: at + bit - 2 * bit * ((at // bit) % 2)}

    def place(c, hop, side):
        return ext.at[c, :, pl.ds((2 - hop) * plane + side * rows, rows), :]

    def in_copy(kind, src, dst, c, device):
        return remote(src, dst, in_send.at[kind, c], in_recv.at[kind, c], device)

    def kv_across(c):
        return in_copy(0, kv_ref.at[theirs + c], place(c, 0, x), c, across)

    def q_across(c):
        return in_copy(1, q_ref.at[theirs + c], qq.at[c, pl.ds(2 * x, 2)], c, across)

    def g_across(c):
        return in_copy(2, g_ref.at[theirs + c], gg.at[c, pl.ds(2 * x, 2)], c, across)

    def own_up(c):
        return in_copy(3, kv_ref.at[mine + c], place(c, 1, x), c, above)

    def other_up(c):
        return in_copy(4, place(c, 0, 1 - x), place(c, 1, 1 - x), c, above)

    def own_on(c):
        return in_copy(5, place(c, 1, x), place(c, 2, x), c, above)

    def other_on(c):
        return in_copy(6, place(c, 1, 1 - x), place(c, 2, 1 - x), c, above)

    def far_copy(c, s):
        return remote(far.at[c, s], far_in.at[c, s], far_send.at[c, s], far_recv.at[c, s], below)

    def near_copy(c):
        return remote(near.at[c], near_in.at[c], near_send.at[c], near_recv.at[c], below)

    def dq_copy(c, i):
        return remote(dq_send.at[c, 2 * (1 - x) + i], dq_ref.at[mine + c, i],
                      dq_ssem.at[c, i], dq_rsem.at[c, i], across)

    def dkv_copy(c):
        return remote(dkv_send.at[c], dkv_ref.at[mine + c], dkv_ssem.at[c], dkv_rsem.at[c],
                      across)

    def count_copy(k):
        return remote(count.at[k], count_in.at[k], count_send.at[k], count_recv.at[k],
                      partner(*bits[k]))

    def mark_copy(hop, side):
        k = 2 * hop + side
        return remote(mark_ref, marks.at[2 * hop + x], mark_send.at[k], mark_recv.at[2 * hop + x],
                      {"ctx": 2 * (p + hop) + side})

    def mark_arrival(hop, side):
        k = 2 * hop + side
        return remote(mark_ref, marks.at[k], mark_send.at[k], mark_recv.at[k],
                      {"ctx": 2 * (p + hop) + side})

    barrier = pltpu.get_barrier_semaphore()

    def greet(device):
        pl.semaphore_signal(barrier, inc=1, device_id=device,
                            device_id_type=pl.DeviceIdType.MESH)

    greet(across)
    for hop in (1, 2):
        for side in (0, 1):
            @pl.when(p + hop < planes)
            def _():
                greet({"ctx": 2 * (p + hop) + side})

            @pl.when(p >= hop)
            def _():
                greet({"ctx": 2 * (p - hop) + side})
    distant = [b for b in bits if b[0] == "dp" or b[1] > 4]
    for b in distant:
        greet(partner(*b))
    pl.semaphore_wait(
        barrier,
        1 + 2 * jnp.minimum(p, 2) + 2 * jnp.minimum(planes - 1 - p, 2) + len(distant),
    )

    kv_across(0).start()

    @pl.when(up)
    def _():
        own_up(0).start()

    mark_ref[...] = jnp.broadcast_to(turn_ref[...], mark_ref.shape)
    for side in (0, 1):
        @pl.when(x != side)
        def _():
            mark_copy(0, side).start()
    for hop in (1, 2):
        for side in (0, 1):
            @pl.when(p + hop < planes)
            def _():
                mark_copy(hop, side).start()
    ones = jnp.sum(mask_ref[...].astype(jnp.float32), axis=1, keepdims=True)
    count[0] = jnp.broadcast_to(ones, count.shape[1:])
    count_copy(0).start()
    q_across(0).start()
    g_across(0).start()

    own = (
        pltpu.make_async_copy(q_ref.at[pl.ds(mine, half)], qq.at[:, pl.ds(2 * x, 2)],
                              local_sem.at[0]),
        pltpu.make_async_copy(g_ref.at[pl.ds(mine, half)], gg.at[:, pl.ds(2 * x, 2)],
                              local_sem.at[1]),
        pltpu.make_async_copy(kv_ref.at[pl.ds(mine, half)],
                              ext.at[:, :, pl.ds(2 * plane + x * rows, rows), :],
                              local_sem.at[2]),
    )
    for copy in own:
        copy.start()

    for hop in (1, 2):
        @pl.when(p < hop)
        def _():
            def clear(c, carry):
                ext[c, :, (2 - hop) * plane : (3 - hop) * plane, :] = jnp.zeros(
                    (2, plane, ext.shape[3]), ext.dtype
                )
                return carry

            lax.fori_loop(0, half, clear, 0)

    def pass_up(c):
        kv_across(c).wait_recv()

        @pl.when(up)
        def _():
            other_up(c).start()

    def more(c):
        kv_across(c).start()

        @pl.when(up)
        def _():
            own_up(c).start()

    def more_q(c):
        q_across(c).start()
        g_across(c).start()

    def pass_on(copy_in, copy_on, c):
        @pl.when(down)
        def _():
            copy_in(c).wait_recv()

            @pl.when(up)
            def _():
                copy_on(c).start()

    def counted(k):
        count_copy(k).wait_recv()
        count[k + 1] = count[k] + count_in[k]
        if k + 1 < len(bits):
            count_copy(k + 1).start()

    def marks_here(hop):
        for side in (0, 1):
            at = ((2 - hop) * plane + side * rows) // STRIP * STRIP
            k = 2 * hop + side

            def lay(source):
                for part in range(rows // STRIP):
                    line = source[part * STRIP : (part + 1) * STRIP]
                    column[at + part * STRIP : at + (part + 1) * STRIP, :] = jnp.transpose(
                        jnp.broadcast_to(line[None], (STRIP, STRIP))
                    )

            present = (x != side) if hop == 0 else (p >= hop)

            @pl.when(present)
            def _():
                mark_arrival(hop, side).wait_recv()
                lay(marks[k, 0].astype(jnp.float32))

            @pl.when(jnp.logical_not(present))
            def _():
                if hop == 0:
                    marks[k] = mark_ref[...]
                    lay(mark_ref[0].astype(jnp.float32))
                else:
                    column[at : at + rows, :] = jnp.full((rows, STRIP), -1.0, jnp.float32)

    def fill_bias(strip):
        low = strip * STRIP
        turn = marks[low // rows, 0:1, low % rows : low % rows + STRIP].astype(jnp.float32)
        row = lax.broadcasted_iota(jnp.int32, (SPAN, STRIP), 1)
        col = lax.broadcasted_iota(jnp.int32, (SPAN, STRIP), 0)
        ok = (column[low : low + SPAN, :] == turn) & (col > row) & (col <= row + WINDOW)
        one = jnp.where(ok, 0.0, MASKED)
        for g in range(bias.shape[2] // STRIP):
            bias[strip, :, g * STRIP : (g + 1) * STRIP] = one

    pass_up(0)
    if half > 1:
        more(1)
    counted(0)
    pass_on(own_up, own_on, 0)
    for hop in (0, 1, 2):
        marks_here(hop)
    counted(1)
    fill_bias(0)
    pass_on(other_up, other_on, 0)
    fill_bias(1)
    if half > 1:
        pass_up(1)
        more_q(1)
    fill_bias(2)
    fill_bias(3)
    for k in range(2, len(bits)):
        counted(k)
    for copy in own:
        copy.wait()

    factor = (rows * n * pairs) / count[len(bits), 0:1, 0:1]

    def finish(c):
        slot = c % 2

        @pl.when(up)
        def _():
            near_copy(c).wait_recv()
            for kind in (0, 1):
                acc[slot, kind, 2 * plane :] += near_in[c, kind].astype(jnp.float32)

        for kind in (0, 1):
            scale = factor * SCALE if kind == 0 else factor
            kept = acc[slot, kind, pl.ds(2 * plane + x * rows, rows), :]
            dkv_ref[mine + c, kind] = (kept * scale).astype(dkv_ref.dtype)
            given = acc[slot, kind, pl.ds(2 * plane + (1 - x) * rows, rows), :]
            dkv_send[c, kind] = (given * scale).astype(dkv_send.dtype)
        dkv_copy(c).start()

    def step(c, carry):
        slot = c % 2
        q_across(c).wait_recv()
        g_across(c).wait_recv()

        @pl.when(p >= 2)
        def _():
            own_on(c).wait_recv()
            other_on(c).wait_recv()

        @pl.when(c + 2 < half)
        def _():
            more(c + 2)

        for s in range(strips):
            strip_grads(c, s, slot, qq, gg, ext, bias, acc, factor, dq_send)
            side, i = s // 2, s % 2

            @pl.when(p >= 2)
            def _():
                far[c, s] = acc[slot, :, s * STRIP : (s + 1) * STRIP, :].astype(far.dtype)
                far_copy(c, s).start()

            @pl.when(x == side)
            def _():
                dq_ref[mine + c, i] = dq_send[c, s]

            @pl.when(x != side)
            def _():
                dq_copy(c, i).start()

            if s == 1:
                @pl.when(c + 1 < half)
                def _():
                    pass_on(own_up, own_on, c + 1)
            if s == 2:
                @pl.when(c + 2 < half)
                def _():
                    pass_up(c + 2)
                    more_q(c + 2)

                @pl.when(c >= 1)
                def _():
                    finish(c - 1)

        @pl.when(c + 1 < half)
        def _():
            pass_on(other_up, other_on, c + 1)

        @pl.when(down)
        def _():
            @pl.when(up)
            def _():
                for s in range(strips):
                    far_copy(c, s).wait_recv()
                    at = plane + s * STRIP
                    near[c, :, s * STRIP : (s + 1) * STRIP, :] = (
                        acc[slot, :, at : at + STRIP, :] + far_in[c, s].astype(jnp.float32)
                    ).astype(near.dtype)

            @pl.when(jnp.logical_not(up))
            def _():
                near[c] = acc[slot, :, plane : 2 * plane, :].astype(near.dtype)

            near_copy(c).start()

        return carry

    lax.fori_loop(0, half, step, 0)
    finish(half - 1)

    def drain(c, carry):
        kv_across(c).wait_send()
        q_across(c).wait_send()
        g_across(c).wait_send()
        for i in range(2):
            dq_copy(c, i).wait()
        dkv_copy(c).wait()

        @pl.when(up)
        def _():
            own_up(c).wait_send()
            other_up(c).wait_send()

            @pl.when(down)
            def _():
                own_on(c).wait_send()
                other_on(c).wait_send()

        @pl.when(down)
        def _():
            near_copy(c).wait_send()

        @pl.when(p >= 2)
        def _():
            for s in range(strips):
                far_copy(c, s).wait_send()
        return carry

    lax.fori_loop(0, half, drain, 0)
    for side in (0, 1):
        @pl.when(x != side)
        def _():
            mark_copy(0, side).wait_send()
    for hop in (1, 2):
        for side in (0, 1):
            @pl.when(p + hop < planes)
            def _():
                mark_copy(hop, side).wait_send()
    for k in range(len(bits)):
        count_copy(k).wait_send()


def on_device(queries, keys, values, d_out, loss_mask, turn_ids):
    rows, heads_q, depth = queries.shape[1:]
    heads = keys.shape[2]
    half = heads // 2
    group = heads_q // heads
    n = lax.axis_size("ctx")
    plane = 2 * rows
    strips = rows // STRIP
    wide = group * STRIP
    pairs = lax.axis_size("dp")
    rounds = n.bit_length() + pairs.bit_length() - 2

    def by_strip(array):
        array = array.reshape(strips, STRIP, heads, group, depth)
        return array.transpose(2, 0, 3, 1, 4).reshape(heads, strips, wide, depth)

    q = by_strip(queries[0])
    g = by_strip(d_out[0] * loss_mask[0][:, None, None].astype(jnp.bfloat16))
    kv = jnp.stack([keys[0], values[0]]).transpose(2, 0, 1, 3)
    vmem = pl.BlockSpec(memory_space=pltpu.VMEM)
    anywhere = pl.BlockSpec(memory_space=pl.ANY)
    bf16, f32 = jnp.bfloat16, jnp.float32
    dma = pltpu.SemaphoreType.DMA
    dq, dkv = pl.pallas_call(
        functools.partial(kernel, n, pairs, rows),
        out_shape=(
            jax.ShapeDtypeStruct((heads, strips, wide, depth), bf16),
            jax.ShapeDtypeStruct((heads, 2, rows, depth), bf16),
        ),
        in_specs=[anywhere] * 3 + [vmem] * 2,
        out_specs=(vmem, vmem),
        scratch_shapes=[
            pltpu.VMEM((half, 2, WINDOW + plane, depth), bf16),
            pltpu.VMEM((half, 2 * strips, wide, depth), bf16),
            pltpu.VMEM((half, 2 * strips, wide, depth), bf16),
            pltpu.VMEM((2, 2, WINDOW + plane, depth), f32),
            pltpu.VMEM((2 * strips, SPAN, wide), f32),
            pltpu.VMEM((WINDOW + plane, STRIP), f32),
            pltpu.VMEM((half, 2 * strips, wide, depth), bf16),
            pltpu.VMEM((half, 2, rows, depth), bf16),
            pltpu.VMEM((half, 2 * strips, 2, STRIP, depth), bf16),
            pltpu.VMEM((half, 2 * strips, 2, STRIP, depth), bf16),
            pltpu.VMEM((half, 2, plane, depth), bf16),
            pltpu.VMEM((half, 2, plane, depth), bf16),
            pltpu.VMEM((8, rows), jnp.int32),
            pltpu.VMEM((6, 8, rows), jnp.int32),
            pltpu.VMEM((rounds + 1, 8, 128), f32),
            pltpu.VMEM((rounds, 8, 128), f32),
            dma((6,)),
            dma((6,)),
            dma((rounds,)),
            dma((rounds,)),
            dma((3,)),
            dma((7, half)),
            dma((7, half)),
            dma((half, 2 * strips)),
            dma((half, 2 * strips)),
            dma((half,)),
            dma((half,)),
            dma((half, 2)),
            dma((half, 2)),
            dma((half,)),
            dma((half,)),
        ],
        compiler_params=pltpu.CompilerParams(
            collective_id=0, has_side_effects=True, vmem_limit_bytes=56 << 20
        ),
    )(q, g, kv, turn_ids, loss_mask)
    dq = dq.reshape(heads, strips, group, STRIP, depth).transpose(1, 3, 0, 2, 4)
    d_queries = dq.reshape(1, rows, heads_q, depth)
    d_keys = dkv[:, 0].transpose(1, 0, 2)[None]
    d_values = dkv[:, 1].transpose(1, 0, 2)[None]
    return (d_queries, d_keys, d_values)


def solution(mesh):
    spec = P("dp", "ctx", "head", None)
    return jax.shard_map(
        on_device,
        mesh=mesh,
        in_specs=(spec, spec, spec, spec, P("dp", "ctx"), P("dp", "ctx")),
        out_specs=(spec, spec, spec),
        check_vma=False,
    )
```

```python
import functools
import math

import jax
import jax.numpy as jnp
from jax import lax
from jax.experimental import pallas as pl
from jax.experimental.pallas import tpu as pltpu
from jax.sharding import PartitionSpec as P

WINDOW = 1024
SCALE = 168.0 ** (-0.5)
STRIP = 128
SPAN = WINDOW + STRIP
MASKED = -1e30


def strip_grads(c, strip, slot, qq, gg, ext, bias, acc, factor, dq_send):
    low = strip * STRIP
    query = qq[c, strip]
    grad = gg[c, strip]
    key = ext[c, 0, low : low + SPAN, :]
    value = ext[c, 1, low : low + SPAN, :]
    logits = lax.dot_general(
        key, query, (((1,), (1,)), ((), ())), preferred_element_type=jnp.float32
    )
    logits = logits * (SCALE * math.log2(math.e)) + bias[strip]
    top = jnp.max(logits, axis=0, keepdims=True)
    raised = jnp.exp2(logits - top)
    prob = raised * (1.0 / jnp.sum(raised, axis=0, keepdims=True))
    grad_prob = lax.dot_general(
        value, grad, (((1,), (1,)), ((), ())), preferred_element_type=jnp.float32
    )
    delta = jnp.sum(prob * grad_prob, axis=0, keepdims=True)
    grad_logit = (prob * (grad_prob - delta)).astype(jnp.bfloat16)
    dq = lax.dot_general(
        grad_logit, key, (((0,), (0,)), ((), ())), preferred_element_type=jnp.float32
    )
    dq_send[c, strip] = (dq * (factor * SCALE)).astype(jnp.bfloat16)
    parts = (
        jnp.dot(grad_logit, query, preferred_element_type=jnp.float32),
        jnp.dot(prob.astype(jnp.bfloat16), grad, preferred_element_type=jnp.float32),
    )
    for kind, part in enumerate(parts):
        if strip == 0:
            acc[slot, kind, :SPAN] = part
        else:
            acc[slot, kind, low : low + WINDOW] += part[:WINDOW]
            acc[slot, kind, low + WINDOW : low + SPAN] = part[WINDOW:]


def kernel(
    n, pairs, rows, q_ref, g_ref, kv_ref, turn_ref, mask_ref,
    dq_ref, dkv_ref,
    ext, qq, gg, acc, bias, column, dq_send, dkv_send, far, far_in, near, near_in,
    mark_ref, marks, count, count_in,
    mark_send, mark_recv, count_send, count_recv, local_sem,
    kv_send, kv_recv, q_send, q_recv, far_send, far_recv, near_send, near_recv,
    dq_ssem, dq_rsem, dkv_ssem, dkv_rsem,
):
    heads = kv_ref.shape[0]
    half = heads // 2
    plane = 2 * rows
    planes = n // 2
    strips = plane // STRIP
    me = lax.axis_index("ctx")
    x = me % 2
    p = me // 2
    up, down = p + 1 < planes, p >= 1
    mine, theirs = x * half, (1 - x) * half
    bits = [("ctx", 1 << b) for b in range(n.bit_length() - 1)]
    bits += [("dp", 1 << b) for b in range(pairs.bit_length() - 1)]
    across, above, below = {"ctx": me + 1 - 2 * x}, {"ctx": me + 2}, {"ctx": me - 2}

    def remote(src, dst, send, recv, device):
        return pltpu.make_async_remote_copy(
            src_ref=src, dst_ref=dst, send_sem=send, recv_sem=recv,
            device_id=device, device_id_type=pl.DeviceIdType.MESH,
        )

    def partner(axis, bit):
        at = lax.axis_index(axis)
        return {axis: at + bit - 2 * bit * ((at // bit) % 2)}

    def place(c, hop, side, kind):
        return ext.at[c, kind, pl.ds((2 - hop) * plane + side * rows, rows), :]

    def kv_copy(what, src, dst, c, kind, device):
        return remote(src, dst, kv_send.at[what, c, kind], kv_recv.at[what, c, kind], device)

    def kv_across(c, kind):
        return kv_copy(0, kv_ref.at[theirs + c, kind], place(c, 0, x, kind), c, kind, across)

    def own_up(c, kind):
        return kv_copy(1, kv_ref.at[mine + c, kind], place(c, 1, x, kind), c, kind, above)

    def other_up(c, kind):
        return kv_copy(2, place(c, 0, 1 - x, kind), place(c, 1, 1 - x, kind), c, kind, above)

    def own_on(c, kind):
        return kv_copy(3, place(c, 1, x, kind), place(c, 2, x, kind), c, kind, above)

    def other_on(c, kind):
        return kv_copy(4, place(c, 1, 1 - x, kind), place(c, 2, 1 - x, kind), c, kind, above)

    def q_across(c):
        return remote(q_ref.at[theirs + c], qq.at[c, pl.ds(2 * x, 2)],
                      q_send.at[0, c], q_recv.at[0, c], across)

    def g_across(c):
        return remote(g_ref.at[theirs + c], gg.at[c, pl.ds(2 * x, 2)],
                      q_send.at[1, c], q_recv.at[1, c], across)

    def far_copy(c, s):
        return remote(far.at[c, s], far_in.at[c, s], far_send.at[c, s], far_recv.at[c, s], below)

    def near_copy(c, s):
        return remote(near.at[c, s], near_in.at[c, s], near_send.at[c, s], near_recv.at[c, s],
                      below)

    def dq_copy(c, i):
        return remote(dq_send.at[c, 2 * (1 - x) + i], dq_ref.at[mine + c, i],
                      dq_ssem.at[c, i], dq_rsem.at[c, i], across)

    def dkv_copy(c, i):
        return remote(dkv_send.at[c, 2 * (1 - x) + i],
                      dkv_ref.at[mine + c, :, pl.ds(i * STRIP, STRIP), :],
                      dkv_ssem.at[c, i], dkv_rsem.at[c, i], across)

    def count_copy(k):
        return remote(count.at[k], count_in.at[k], count_send.at[k], count_recv.at[k],
                      partner(*bits[k]))

    def mark_copy(hop, side):
        k = 2 * hop + side
        return remote(mark_ref, marks.at[2 * hop + x], mark_send.at[k], mark_recv.at[2 * hop + x],
                      {"ctx": 2 * (p + hop) + side})

    def mark_arrival(hop, side):
        k = 2 * hop + side
        return remote(mark_ref, marks.at[k], mark_send.at[k], mark_recv.at[k],
                      {"ctx": 2 * (p + hop) + side})

    barrier = pltpu.get_barrier_semaphore()

    def greet(device):
        pl.semaphore_signal(barrier, inc=1, device_id=device,
                            device_id_type=pl.DeviceIdType.MESH)

    greet(across)
    for hop in (1, 2):
        for side in (0, 1):
            @pl.when(p + hop < planes)
            def _():
                greet({"ctx": 2 * (p + hop) + side})

            @pl.when(p >= hop)
            def _():
                greet({"ctx": 2 * (p - hop) + side})
    distant = [b for b in bits if b[0] == "dp" or b[1] > 4]
    for b in distant:
        greet(partner(*b))
    pl.semaphore_wait(
        barrier,
        1 + 2 * jnp.minimum(p, 2) + 2 * jnp.minimum(planes - 1 - p, 2) + len(distant),
    )

    def give(c):
        for kind in (0, 1):
            kv_across(c, kind).start()

    def give_q(c):
        q_across(c).start()
        g_across(c).start()

    def send_own(c):
        @pl.when(up)
        def _():
            for kind in (0, 1):
                own_up(c, kind).start()

    def pass_up(c):
        for kind in (0, 1):
            kv_across(c, kind).wait_recv()

            @pl.when(up)
            def _():
                other_up(c, kind).start()

    def pass_on(copy_in, copy_on, c):
        @pl.when(down)
        def _():
            for kind in (0, 1):
                copy_in(c, kind).wait_recv()

                @pl.when(up)
                def _():
                    copy_on(c, kind).start()

    give(0)
    send_own(0)
    mark_ref[...] = jnp.broadcast_to(turn_ref[...], mark_ref.shape)
    for side in (0, 1):
        @pl.when(x != side)
        def _():
            mark_copy(0, side).start()
    for hop in (1, 2):
        for side in (0, 1):
            @pl.when(p + hop < planes)
            def _():
                mark_copy(hop, side).start()
    ones = jnp.sum(mask_ref[...].astype(jnp.float32), axis=1, keepdims=True)
    count[0] = jnp.broadcast_to(ones, count.shape[1:])
    count_copy(0).start()
    for c in range(1, half):
        give(c)
        give_q(c - 1)
    give_q(half - 1)

    own = (
        pltpu.make_async_copy(q_ref.at[pl.ds(mine, half)], qq.at[:, pl.ds(2 * x, 2)],
                              local_sem.at[0]),
        pltpu.make_async_copy(g_ref.at[pl.ds(mine, half)], gg.at[:, pl.ds(2 * x, 2)],
                              local_sem.at[1]),
        pltpu.make_async_copy(kv_ref.at[pl.ds(mine, half)],
                              ext.at[:, :, pl.ds(2 * plane + x * rows, rows), :],
                              local_sem.at[2]),
    )
    for copy in own:
        copy.start()

    for hop in (1, 2):
        @pl.when(p < hop)
        def _():
            def clear(c, carry):
                ext[c, :, (2 - hop) * plane : (3 - hop) * plane, :] = jnp.zeros(
                    (2, plane, ext.shape[3]), ext.dtype
                )
                return carry

            lax.fori_loop(0, half, clear, 0)

    def counted(k):
        count_copy(k).wait_recv()
        count[k + 1] = count[k] + count_in[k]
        if k + 1 < len(bits):
            count_copy(k + 1).start()

    def marks_here(hop):
        for side in (0, 1):
            at = ((2 - hop) * plane + side * rows) // STRIP * STRIP
            k = 2 * hop + side

            def lay(source):
                for part in range(rows // STRIP):
                    line = source[part * STRIP : (part + 1) * STRIP]
                    column[at + part * STRIP : at + (part + 1) * STRIP, :] = jnp.transpose(
                        jnp.broadcast_to(line[None], (STRIP, STRIP))
                    )

            present = (x != side) if hop == 0 else (p >= hop)

            @pl.when(present)
            def _():
                mark_arrival(hop, side).wait_recv()
                lay(marks[k, 0].astype(jnp.float32))

            @pl.when(jnp.logical_not(present))
            def _():
                if hop == 0:
                    marks[k] = mark_ref[...]
                    lay(mark_ref[0].astype(jnp.float32))
                else:
                    column[at : at + rows, :] = jnp.full((rows, STRIP), -1.0, jnp.float32)

    def fill_bias(strip):
        low = strip * STRIP
        turn = marks[low // rows, 0:1, low % rows : low % rows + STRIP].astype(jnp.float32)
        row = lax.broadcasted_iota(jnp.int32, (SPAN, STRIP), 1)
        col = lax.broadcasted_iota(jnp.int32, (SPAN, STRIP), 0)
        ok = (column[low : low + SPAN, :] == turn) & (col > row) & (col <= row + WINDOW)
        one = jnp.where(ok, 0.0, MASKED)
        for g in range(bias.shape[2] // STRIP):
            bias[strip, :, g * STRIP : (g + 1) * STRIP] = one

    pass_up(0)
    counted(0)
    for hop in (0, 1, 2):
        marks_here(hop)
    fill_bias(0)
    counted(1)
    fill_bias(1)
    pass_on(own_up, own_on, 0)
    fill_bias(2)
    fill_bias(3)
    for k in range(2, len(bits)):
        counted(k)
    pass_on(other_up, other_on, 0)
    send_own(1)
    pass_up(1)
    for copy in own:
        copy.wait()

    factor = (rows * n * pairs) / count[len(bits), 0:1, 0:1]

    def pass_back(c):
        @pl.when(down)
        def _():
            for s in range(strips):
                at = plane + s * STRIP

                @pl.when(up)
                def _():
                    far_copy(c, s).wait_recv()
                    near[c, s] = (
                        acc[c % 2, :, at : at + STRIP, :] + far_in[c, s].astype(jnp.float32)
                    ).astype(near.dtype)

                @pl.when(jnp.logical_not(up))
                def _():
                    near[c, s] = acc[c % 2, :, at : at + STRIP, :].astype(near.dtype)

                near_copy(c, s).start()

    def finish(c):
        for s in range(strips):
            side, i = s // 2, s % 2
            at = 2 * plane + s * STRIP

            @pl.when(up)
            def _():
                near_copy(c, s).wait_recv()
                acc[c % 2, :, at : at + STRIP, :] += near_in[c, s].astype(jnp.float32)

            for kind in (0, 1):
                scale = factor * SCALE if kind == 0 else factor
                dkv_send[c, s, kind] = (
                    acc[c % 2, kind, at : at + STRIP, :] * scale
                ).astype(dkv_send.dtype)

            @pl.when(x == side)
            def _():
                dkv_ref[mine + c, :, i * STRIP : (i + 1) * STRIP, :] = dkv_send[c, s]

            @pl.when(x != side)
            def _():
                dkv_copy(c, i).start()

    def step(c, carry):
        @pl.when(c >= 1)
        def _():
            pass_back(c - 1)

        q_across(c).wait_recv()
        g_across(c).wait_recv()

        @pl.when(p >= 2)
        def _():
            for kind in (0, 1):
                own_on(c, kind).wait_recv()
                other_on(c, kind).wait_recv()

        for s in range(strips):
            strip_grads(c, s, c % 2, qq, gg, ext, bias, acc, factor, dq_send)
            side, i = s // 2, s % 2

            @pl.when(p >= 2)
            def _():
                far[c, s] = acc[c % 2, :, s * STRIP : (s + 1) * STRIP, :].astype(far.dtype)
                far_copy(c, s).start()

            @pl.when(x == side)
            def _():
                dq_ref[mine + c, i] = dq_send[c, s]

            @pl.when(x != side)
            def _():
                dq_copy(c, i).start()

            if s == 1:
                @pl.when(c + 1 < half)
                def _():
                    pass_on(own_up, own_on, c + 1)

        @pl.when(c + 1 < half)
        def _():
            pass_on(other_up, other_on, c + 1)

        @pl.when(c + 2 < half)
        def _():
            send_own(c + 2)
            pass_up(c + 2)

        @pl.when(c >= 1)
        def _():
            finish(c - 1)

        return carry

    lax.fori_loop(0, half, step, 0)
    pass_back(half - 1)
    finish(half - 1)

    def drain(c, carry):
        q_across(c).wait_send()
        g_across(c).wait_send()
        for i in range(2):
            dq_copy(c, i).wait()
            dkv_copy(c, i).wait()
        for kind in (0, 1):
            kv_across(c, kind).wait_send()

            @pl.when(up)
            def _():
                own_up(c, kind).wait_send()
                other_up(c, kind).wait_send()

                @pl.when(down)
                def _():
                    own_on(c, kind).wait_send()
                    other_on(c, kind).wait_send()

        for s in range(strips):
            @pl.when(down)
            def _():
                near_copy(c, s).wait_send()

            @pl.when(p >= 2)
            def _():
                far_copy(c, s).wait_send()
        return carry

    lax.fori_loop(0, half, drain, 0)
    for side in (0, 1):
        @pl.when(x != side)
        def _():
            mark_copy(0, side).wait_send()
    for hop in (1, 2):
        for side in (0, 1):
            @pl.when(p + hop < planes)
            def _():
                mark_copy(hop, side).wait_send()
    for k in range(len(bits)):
        count_copy(k).wait_send()


def on_device(queries, keys, values, d_out, loss_mask, turn_ids):
    rows, heads_q, depth = queries.shape[1:]
    heads = keys.shape[2]
    half = heads // 2
    group = heads_q // heads
    n = lax.axis_size("ctx")
    plane = 2 * rows
    strips = rows // STRIP
    wide = group * STRIP
    pairs = lax.axis_size("dp")
    rounds = n.bit_length() + pairs.bit_length() - 2

    def by_strip(array):
        array = array.reshape(strips, STRIP, heads, group, depth)
        return array.transpose(2, 0, 3, 1, 4).reshape(heads, strips, wide, depth)

    q = by_strip(queries[0])
    g = by_strip(d_out[0] * loss_mask[0][:, None, None].astype(jnp.bfloat16))
    kv = jnp.stack([keys[0], values[0]]).transpose(2, 0, 1, 3)
    vmem = pl.BlockSpec(memory_space=pltpu.VMEM)
    anywhere = pl.BlockSpec(memory_space=pl.ANY)
    bf16, f32 = jnp.bfloat16, jnp.float32
    dma = pltpu.SemaphoreType.DMA
    dq, dkv = pl.pallas_call(
        functools.partial(kernel, n, pairs, rows),
        out_shape=(
            jax.ShapeDtypeStruct((heads, strips, wide, depth), bf16),
            jax.ShapeDtypeStruct((heads, 2, rows, depth), bf16),
        ),
        in_specs=[anywhere] * 3 + [vmem] * 2,
        out_specs=(vmem, vmem),
        scratch_shapes=[
            pltpu.VMEM((half, 2, WINDOW + plane, depth), bf16),
            pltpu.VMEM((half, 2 * strips, wide, depth), bf16),
            pltpu.VMEM((half, 2 * strips, wide, depth), bf16),
            pltpu.VMEM((2, 2, WINDOW + plane, depth), f32),
            pltpu.VMEM((2 * strips, SPAN, wide), f32),
            pltpu.VMEM((WINDOW + plane, STRIP), f32),
            pltpu.VMEM((half, 2 * strips, wide, depth), bf16),
            pltpu.VMEM((half, 2 * strips, 2, STRIP, depth), bf16),
            pltpu.VMEM((half, 2 * strips, 2, STRIP, depth), bf16),
            pltpu.VMEM((half, 2 * strips, 2, STRIP, depth), bf16),
            pltpu.VMEM((half, 2 * strips, 2, STRIP, depth), bf16),
            pltpu.VMEM((half, 2 * strips, 2, STRIP, depth), bf16),
            pltpu.VMEM((8, rows), jnp.int32),
            pltpu.VMEM((6, 8, rows), jnp.int32),
            pltpu.VMEM((rounds + 1, 8, 128), f32),
            pltpu.VMEM((rounds, 8, 128), f32),
            dma((6,)),
            dma((6,)),
            dma((rounds,)),
            dma((rounds,)),
            dma((3,)),
            dma((5, half, 2)),
            dma((5, half, 2)),
            dma((2, half)),
            dma((2, half)),
            dma((half, 2 * strips)),
            dma((half, 2 * strips)),
            dma((half, 2 * strips)),
            dma((half, 2 * strips)),
            dma((half, strips)),
            dma((half, strips)),
            dma((half, strips)),
            dma((half, strips)),
        ],
        compiler_params=pltpu.CompilerParams(
            collective_id=0, has_side_effects=True, vmem_limit_bytes=56 << 20
        ),
    )(q, g, kv, turn_ids, loss_mask)
    dq = dq.reshape(heads, strips, group, STRIP, depth).transpose(1, 3, 0, 2, 4)
    d_queries = dq.reshape(1, rows, heads_q, depth)
    d_keys = dkv[:, 0].transpose(1, 0, 2)[None]
    d_values = dkv[:, 1].transpose(1, 0, 2)[None]
    return (d_queries, d_keys, d_values)


def solution(mesh):
    spec = P("dp", "ctx", "head", None)
    return jax.shard_map(
        on_device,
        mesh=mesh,
        in_specs=(spec, spec, spec, spec, P("dp", "ctx"), P("dp", "ctx")),
        out_specs=(spec, spec, spec),
        check_vma=False,
    )
```

```python
import functools
import math

import jax
import jax.numpy as jnp
from jax import lax
from jax.experimental import pallas as pl
from jax.experimental.pallas import tpu as pltpu
from jax.sharding import PartitionSpec as P

WINDOW = 1024
SCALE = 168.0 ** (-0.5)
STRIP = 128
SPAN = WINDOW + STRIP
MASKED = -1e30


def strip_grads(c, strip, slot, qq, gg, ext, bias, token, acc, factor, dq_send):
    low = strip * STRIP
    side, i = low // qq.shape[2], low % qq.shape[2]
    wide = (STRIP * qq.shape[3], qq.shape[4])
    query = qq[c, side, i : i + STRIP].reshape(wide)
    grad = gg[c, side, i : i + STRIP].reshape(wide)
    key = ext[c, 0, low : low + SPAN, :]
    value = ext[c, 1, low : low + SPAN, :]
    logits = lax.dot_general(
        key, query, (((1,), (1,)), ((), ())), preferred_element_type=jnp.float32
    )
    logits = logits * (SCALE * math.log2(math.e)) + bias[strip]
    top = jnp.max(logits, axis=0, keepdims=True)
    raised = jnp.exp2(logits - top)
    prob = raised * (token[strip, 1:2, :] / jnp.sum(raised, axis=0, keepdims=True))
    grad_prob = lax.dot_general(
        value, grad, (((1,), (1,)), ((), ())), preferred_element_type=jnp.float32
    )
    delta = jnp.sum(prob * grad_prob, axis=0, keepdims=True)
    grad_logit = (prob * (grad_prob - delta)).astype(jnp.bfloat16)
    dq = lax.dot_general(
        grad_logit, key, (((0,), (0,)), ((), ())), preferred_element_type=jnp.float32
    )
    dq = (dq * (factor * SCALE)).astype(jnp.bfloat16)
    dq_send[c, strip] = dq.reshape(dq_send.shape[2:])
    parts = (
        jnp.dot(grad_logit, query, preferred_element_type=jnp.float32),
        jnp.dot(prob.astype(jnp.bfloat16), grad, preferred_element_type=jnp.float32),
    )
    for kind, part in enumerate(parts):
        if strip == 0:
            acc[slot, kind, :SPAN] = part
        else:
            acc[slot, kind, low : low + WINDOW] += part[:WINDOW]
            acc[slot, kind, low + WINDOW : low + SPAN] = part[WINDOW:]


def kernel(
    n, pairs, rows, q_ref, g_ref, k_ref, v_ref, turn_ref, mask_ref,
    dq_ref, dk_ref, dv_ref,
    raw, kv_ref, ext, qq, gg, acc, bias, token, column, dq_send, dkv_send, far, far_in, near, near_in,
    mark_ref, marks, count, count_in,
    mark_send, mark_recv, count_send, count_recv, local_sem, own_sem, keep_sem,
    kv_send, kv_recv, q_send, q_recv, far_send, far_recv, near_send, near_recv,
    dq_ssem, dq_rsem, dkv_ssem, dkv_rsem,
):
    heads, group = q_ref.shape[1:3]
    half = heads // 2
    plane = 2 * rows
    planes = n // 2
    strips = plane // STRIP
    me = lax.axis_index("ctx")
    x = me % 2
    p = me // 2
    up, down = p + 1 < planes, p >= 1
    mine, theirs = x * half, (1 - x) * half
    bits = [("ctx", 1 << b) for b in range(n.bit_length() - 1)]
    bits += [("dp", 1 << b) for b in range(pairs.bit_length() - 1)]
    across, above, below = {"ctx": me + 1 - 2 * x}, {"ctx": me + 2}, {"ctx": me - 2}

    def remote(src, dst, send, recv, device):
        return pltpu.make_async_remote_copy(
            src_ref=src, dst_ref=dst, send_sem=send, recv_sem=recv,
            device_id=device, device_id_type=pl.DeviceIdType.MESH,
        )

    def partner(axis, bit):
        at = lax.axis_index(axis)
        return {axis: at + bit - 2 * bit * ((at // bit) % 2)}

    def place(c, hop, side, kind):
        return ext.at[c, kind, pl.ds((2 - hop) * plane + side * rows, rows), :]

    def kv_copy(what, src, dst, c, kind, device):
        return remote(src, dst, kv_send.at[what, c, kind], kv_recv.at[what, c, kind], device)

    def kv_across(c, kind):
        return kv_copy(0, kv_ref.at[theirs + c, kind], place(c, 0, x, kind), c, kind, across)

    def own_up(c, kind):
        return kv_copy(1, kv_ref.at[mine + c, kind], place(c, 1, x, kind), c, kind, above)

    def other_up(c, kind):
        return kv_copy(2, place(c, 0, 1 - x, kind), place(c, 1, 1 - x, kind), c, kind, above)

    def own_on(c, kind):
        return kv_copy(3, place(c, 1, x, kind), place(c, 2, x, kind), c, kind, above)

    def other_on(c, kind):
        return kv_copy(4, place(c, 1, 1 - x, kind), place(c, 2, 1 - x, kind), c, kind, above)

    def q_across(c):
        return remote(q_ref.at[:, theirs + c], qq.at[c, x],
                      q_send.at[0, c], q_recv.at[0, c], across)

    def g_across(c):
        return remote(g_ref.at[:, theirs + c], gg.at[c, x],
                      q_send.at[1, c], q_recv.at[1, c], across)

    def far_copy(c, s):
        return remote(far.at[c, s], far_in.at[c, s], far_send.at[c, s], far_recv.at[c, s], below)

    def near_copy(c, s):
        return remote(near.at[c, s], near_in.at[c, s], near_send.at[c, s], near_recv.at[c, s],
                      below)

    def dq_copy(c, i):
        return remote(dq_send.at[c, 2 * (1 - x) + i],
                      dq_ref.at[pl.ds(i * STRIP, STRIP), mine + c],
                      dq_ssem.at[c, i], dq_rsem.at[c, i], across)

    def dq_keep(c, i):
        return pltpu.make_async_copy(dq_send.at[c, 2 * x + i],
                                     dq_ref.at[pl.ds(i * STRIP, STRIP), mine + c],
                                     keep_sem.at[c, i])

    def dkv_copy(c, i, kind):
        return remote(dkv_send.at[c, 2 * (1 - x) + i, kind],
                      (dk_ref, dv_ref)[kind].at[mine + c, pl.ds(i * STRIP, STRIP), :],
                      dkv_ssem.at[c, i, kind], dkv_rsem.at[c, i, kind], across)

    def count_copy(k):
        return remote(count.at[k], count_in.at[k], count_send.at[k], count_recv.at[k],
                      partner(*bits[k]))

    def mark_copy(hop, side):
        k = 2 * hop + side
        return remote(mark_ref, marks.at[2 * hop + x], mark_send.at[k], mark_recv.at[2 * hop + x],
                      {"ctx": 2 * (p + hop) + side})

    def mark_arrival(hop, side):
        k = 2 * hop + side
        return remote(mark_ref, marks.at[k], mark_send.at[k], mark_recv.at[k],
                      {"ctx": 2 * (p + hop) + side})

    raw_copies = [
        pltpu.make_async_copy(ref, raw.at[kind], local_sem.at[kind])
        for kind, ref in enumerate((k_ref, v_ref))
    ]
    own = [
        pltpu.make_async_copy(ref.at[:, mine + c], buffer.at[c, x], own_sem.at[kind, c])
        for c in range(half)
        for kind, (ref, buffer) in enumerate(((q_ref, qq), (g_ref, gg)))
    ]
    for copy in raw_copies:
        copy.start()
    barrier = pltpu.get_barrier_semaphore()

    def greet(device):
        pl.semaphore_signal(barrier, inc=1, device_id=device,
                            device_id_type=pl.DeviceIdType.MESH)

    greet(across)
    for hop in (1, 2):
        for side in (0, 1):
            @pl.when(p + hop < planes)
            def _():
                greet({"ctx": 2 * (p + hop) + side})

            @pl.when(p >= hop)
            def _():
                greet({"ctx": 2 * (p - hop) + side})
    distant = [b for b in bits if b[0] == "dp" or b[1] > 4]
    for b in distant:
        greet(partner(*b))
    for copy in own:
        copy.start()
    for kind, copy in enumerate(raw_copies):
        copy.wait()
        kv_ref[:, kind] = jnp.swapaxes(raw[kind], 0, 1)
    pl.semaphore_wait(
        barrier,
        1 + 2 * jnp.minimum(p, 2) + 2 * jnp.minimum(planes - 1 - p, 2) + len(distant),
    )

    def give(c):
        for kind in (0, 1):
            kv_across(c, kind).start()

    def give_q(c):
        q_across(c).start()
        g_across(c).start()

    def send_own(c):
        @pl.when(up)
        def _():
            for kind in (0, 1):
                own_up(c, kind).start()

    def pass_up(c):
        for kind in (0, 1):
            kv_across(c, kind).wait_recv()

            @pl.when(up)
            def _():
                other_up(c, kind).start()

    def pass_on(copy_in, copy_on, c):
        @pl.when(down)
        def _():
            for kind in (0, 1):
                copy_in(c, kind).wait_recv()

                @pl.when(up)
                def _():
                    copy_on(c, kind).start()

    give(0)
    send_own(0)
    line = lax.broadcasted_iota(jnp.int32, mark_ref.shape, 0)
    mark_ref[...] = jnp.where(line == 0, turn_ref[...], mask_ref[...])
    for side in (0, 1):
        @pl.when(x != side)
        def _():
            mark_copy(0, side).start()
    for hop in (1, 2):
        for side in (0, 1):
            @pl.when(p + hop < planes)
            def _():
                mark_copy(hop, side).start()
    ones = jnp.sum(mask_ref[...].astype(jnp.float32), axis=1, keepdims=True)
    count[0] = jnp.broadcast_to(ones, count.shape[1:])
    count_copy(0).start()
    for c in range(1, half):
        give(c)
        give_q(c - 1)
    give_q(half - 1)

    own_place = pltpu.make_async_copy(
        kv_ref.at[pl.ds(mine, half)],
        ext.at[:, :, pl.ds(2 * plane + x * rows, rows), :],
        local_sem.at[2],
    )
    own_place.start()

    for hop in (1, 2):
        @pl.when(p < hop)
        def _():
            def clear(c, carry):
                ext[c, :, (2 - hop) * plane : (3 - hop) * plane, :] = jnp.zeros(
                    (2, plane, ext.shape[3]), ext.dtype
                )
                return carry

            lax.fori_loop(0, half, clear, 0)

    def counted(k):
        count_copy(k).wait_recv()
        count[k + 1] = count[k] + count_in[k]
        if k + 1 < len(bits):
            count_copy(k + 1).start()

    def marks_here(hop):
        for side in (0, 1):
            at = ((2 - hop) * plane + side * rows) // STRIP * STRIP
            k = 2 * hop + side

            def lay(source):
                for part in range(rows // STRIP):
                    line = source[part * STRIP : (part + 1) * STRIP]
                    column[at + part * STRIP : at + (part + 1) * STRIP, :] = jnp.transpose(
                        jnp.broadcast_to(line[None], (STRIP, STRIP))
                    )

            present = (x != side) if hop == 0 else (p >= hop)

            @pl.when(present)
            def _():
                mark_arrival(hop, side).wait_recv()
                lay(marks[k, 0].astype(jnp.float32))

            @pl.when(jnp.logical_not(present))
            def _():
                if hop == 0:
                    marks[k] = mark_ref[...]
                    lay(mark_ref[0].astype(jnp.float32))
                else:
                    column[at : at + rows, :] = jnp.full((rows, STRIP), -1.0, jnp.float32)

    shift = group.bit_length() - 1

    def fill_bias(strip):
        low = strip * STRIP
        lines = marks[low // rows, :, low % rows : low % rows + STRIP]
        wide = (STRIP, STRIP * group)
        spread = (
            lax.broadcasted_iota(jnp.int32, wide, 1) >> shift
        ) == lax.broadcasted_iota(jnp.int32, wide, 0)
        token[strip] = jnp.dot(
            lines.astype(jnp.float32).astype(jnp.bfloat16),
            jnp.where(spread, 1.0, 0.0).astype(jnp.bfloat16),
            preferred_element_type=jnp.float32,
        )
        shape = (SPAN, STRIP * group)
        row = lax.broadcasted_iota(jnp.int32, shape, 1) >> shift
        col = lax.broadcasted_iota(jnp.int32, shape, 0)
        turn = jnp.concatenate([column[low : low + SPAN, :]] * group, axis=1)
        ok = (turn == token[strip, 0:1, :]) & (col > row) & (col <= row + WINDOW)
        bias[strip] = jnp.where(ok, 0.0, MASKED)

    pass_up(0)
    counted(0)
    for hop in (0, 1, 2):
        marks_here(hop)
    fill_bias(0)
    counted(1)
    fill_bias(1)
    pass_on(own_up, own_on, 0)
    fill_bias(2)
    fill_bias(3)
    for k in range(2, len(bits)):
        counted(k)
    pass_on(other_up, other_on, 0)
    send_own(1)
    pass_up(1)
    for copy in own:
        copy.wait()
    own_place.wait()

    factor = (rows * n * pairs) / count[len(bits), 0:1, 0:1]

    def pass_back(c):
        @pl.when(down)
        def _():
            for s in range(strips):
                at = plane + s * STRIP

                @pl.when(up)
                def _():
                    far_copy(c, s).wait_recv()
                    near[c, s] = (
                        acc[c % 2, :, at : at + STRIP, :] + far_in[c, s].astype(jnp.float32)
                    ).astype(near.dtype)

                @pl.when(jnp.logical_not(up))
                def _():
                    near[c, s] = acc[c % 2, :, at : at + STRIP, :].astype(near.dtype)

                near_copy(c, s).start()

    def finish(c):
        for s in range(strips):
            side, i = s // 2, s % 2
            at = 2 * plane + s * STRIP

            @pl.when(up)
            def _():
                near_copy(c, s).wait_recv()
                acc[c % 2, :, at : at + STRIP, :] += near_in[c, s].astype(jnp.float32)

            for kind, out in enumerate((dk_ref, dv_ref)):
                scale = factor * SCALE if kind == 0 else factor
                dkv_send[c, s, kind] = (
                    acc[c % 2, kind, at : at + STRIP, :] * scale
                ).astype(dkv_send.dtype)

                @pl.when(x == side)
                def _():
                    out[mine + c, i * STRIP : (i + 1) * STRIP, :] = dkv_send[c, s, kind]

                @pl.when(x != side)
                def _():
                    dkv_copy(c, i, kind).start()

    def step(c, carry):
        @pl.when(c >= 1)
        def _():
            pass_back(c - 1)

        q_across(c).wait_recv()
        g_across(c).wait_recv()

        @pl.when(p >= 2)
        def _():
            for kind in (0, 1):
                own_on(c, kind).wait_recv()
                other_on(c, kind).wait_recv()

        for s in range(strips):
            strip_grads(c, s, c % 2, qq, gg, ext, bias, token, acc, factor, dq_send)
            side, i = s // 2, s % 2

            @pl.when(p >= 2)
            def _():
                far[c, s] = acc[c % 2, :, s * STRIP : (s + 1) * STRIP, :].astype(far.dtype)
                far_copy(c, s).start()

            @pl.when(x == side)
            def _():
                dq_keep(c, i).start()

            @pl.when(x != side)
            def _():
                dq_copy(c, i).start()

            if s == 1:
                @pl.when(c + 1 < half)
                def _():
                    pass_on(own_up, own_on, c + 1)

        @pl.when(c + 1 < half)
        def _():
            pass_on(other_up, other_on, c + 1)

        @pl.when(c + 2 < half)
        def _():
            send_own(c + 2)
            pass_up(c + 2)

        @pl.when(c >= 1)
        def _():
            finish(c - 1)

        return carry

    lax.fori_loop(0, half, step, 0)
    pass_back(half - 1)
    finish(half - 1)

    def drain(c, carry):
        q_across(c).wait_send()
        g_across(c).wait_send()
        for i in range(2):
            dq_keep(c, i).wait()
            dq_copy(c, i).wait()
            for kind in (0, 1):
                dkv_copy(c, i, kind).wait()
        for kind in (0, 1):
            kv_across(c, kind).wait_send()

            @pl.when(up)
            def _():
                own_up(c, kind).wait_send()
                other_up(c, kind).wait_send()

                @pl.when(down)
                def _():
                    own_on(c, kind).wait_send()
                    other_on(c, kind).wait_send()

        for s in range(strips):
            @pl.when(down)
            def _():
                near_copy(c, s).wait_send()

            @pl.when(p >= 2)
            def _():
                far_copy(c, s).wait_send()
        return carry

    lax.fori_loop(0, half, drain, 0)
    for side in (0, 1):
        @pl.when(x != side)
        def _():
            mark_copy(0, side).wait_send()
    for hop in (1, 2):
        for side in (0, 1):
            @pl.when(p + hop < planes)
            def _():
                mark_copy(hop, side).wait_send()
    for k in range(len(bits)):
        count_copy(k).wait_send()


def on_device(queries, keys, values, d_out, loss_mask, turn_ids):
    rows, heads_q, depth = queries.shape[1:]
    heads = keys.shape[2]
    half = heads // 2
    group = heads_q // heads
    n = lax.axis_size("ctx")
    plane = 2 * rows
    strips = rows // STRIP
    wide = group * STRIP
    pairs = lax.axis_size("dp")
    rounds = n.bit_length() + pairs.bit_length() - 2

    def by_group(array):
        return array.reshape(rows, heads, group, depth)

    vmem = pl.BlockSpec(memory_space=pltpu.VMEM)
    anywhere = pl.BlockSpec(memory_space=pl.ANY)
    bf16, f32 = jnp.bfloat16, jnp.float32
    dma = pltpu.SemaphoreType.DMA
    dq, dk, dv = pl.pallas_call(
        functools.partial(kernel, n, pairs, rows),
        out_shape=(
            jax.ShapeDtypeStruct((rows, heads, group, depth), bf16),
            jax.ShapeDtypeStruct((heads, rows, depth), bf16),
            jax.ShapeDtypeStruct((heads, rows, depth), bf16),
        ),
        in_specs=[anywhere] * 4 + [vmem] * 2,
        out_specs=(anywhere, vmem, vmem),
        scratch_shapes=[
            pltpu.VMEM((2, rows, heads, depth), bf16),
            pltpu.VMEM((heads, 2, rows, depth), bf16),
            pltpu.VMEM((half, 2, WINDOW + plane, depth), bf16),
            pltpu.VMEM((half, 2, rows, group, depth), bf16),
            pltpu.VMEM((half, 2, rows, group, depth), bf16),
            pltpu.VMEM((2, 2, WINDOW + plane, depth), f32),
            pltpu.VMEM((2 * strips, SPAN, wide), f32),
            pltpu.VMEM((2 * strips, 8, wide), f32),
            pltpu.VMEM((WINDOW + plane, STRIP), f32),
            pltpu.VMEM((half, 2 * strips, STRIP, group, depth), bf16),
            pltpu.VMEM((half, 2 * strips, 2, STRIP, depth), bf16),
            pltpu.VMEM((half, 2 * strips, 2, STRIP, depth), bf16),
            pltpu.VMEM((half, 2 * strips, 2, STRIP, depth), bf16),
            pltpu.VMEM((half, 2 * strips, 2, STRIP, depth), bf16),
            pltpu.VMEM((half, 2 * strips, 2, STRIP, depth), bf16),
            pltpu.VMEM((8, rows), jnp.int32),
            pltpu.VMEM((6, 8, rows), jnp.int32),
            pltpu.VMEM((rounds + 1, 8, 128), f32),
            pltpu.VMEM((rounds, 8, 128), f32),
            dma((6,)),
            dma((6,)),
            dma((rounds,)),
            dma((rounds,)),
            dma((3,)),
            dma((2, half)),
            dma((half, strips)),
            dma((5, half, 2)),
            dma((5, half, 2)),
            dma((2, half)),
            dma((2, half)),
            dma((half, 2 * strips)),
            dma((half, 2 * strips)),
            dma((half, 2 * strips)),
            dma((half, 2 * strips)),
            dma((half, strips)),
            dma((half, strips)),
            dma((half, strips, 2)),
            dma((half, strips, 2)),
        ],
        compiler_params=pltpu.CompilerParams(
            collective_id=0, has_side_effects=True, vmem_limit_bytes=56 << 20
        ),
    )(by_group(queries[0]), by_group(d_out[0]), keys[0], values[0], turn_ids, loss_mask)
    d_queries = dq.reshape(1, rows, heads_q, depth)
    return (d_queries, dk.transpose(1, 0, 2)[None], dv.transpose(1, 0, 2)[None])


def solution(mesh):
    spec = P("dp", "ctx", "head", None)
    return jax.shard_map(
        on_device,
        mesh=mesh,
        in_specs=(spec, spec, spec, spec, P("dp", "ctx"), P("dp", "ctx")),
        out_specs=(spec, spec, spec),
        check_vma=False,
    )
```

```python
import functools
import math

import jax
import jax.numpy as jnp
from jax import lax
from jax.experimental import pallas as pl
from jax.experimental.pallas import tpu as pltpu
from jax.sharding import PartitionSpec as P

WINDOW = 1024
SCALE = 168.0 ** (-0.5)
STRIP = 128
SPAN = WINDOW + STRIP
MASKED = -1e30


def strip_grads(c, strip, slot, qq, gg, ext, bias, token, acc, factor, dq_send):
    low = strip * STRIP
    side, i = low // qq.shape[2], low % qq.shape[2]
    wide = (STRIP * qq.shape[3], qq.shape[4])
    query = qq[c, side, i : i + STRIP].reshape(wide)
    grad = gg[c, side, i : i + STRIP].reshape(wide)
    key = ext[c, 0, low : low + SPAN, :]
    value = ext[c, 1, low : low + SPAN, :]
    logits = lax.dot_general(
        key, query, (((1,), (1,)), ((), ())), preferred_element_type=jnp.float32
    )
    logits = logits * (SCALE * math.log2(math.e)) + bias[strip]
    top = jnp.max(logits, axis=0, keepdims=True)
    raised = jnp.exp2(logits - top)
    prob = raised * (token[strip, 1:2, :] / jnp.sum(raised, axis=0, keepdims=True))
    grad_prob = lax.dot_general(
        value, grad, (((1,), (1,)), ((), ())), preferred_element_type=jnp.float32
    )
    delta = jnp.sum(prob * grad_prob, axis=0, keepdims=True)
    grad_logit = (prob * (grad_prob - delta)).astype(jnp.bfloat16)
    dq = lax.dot_general(
        grad_logit, key, (((0,), (0,)), ((), ())), preferred_element_type=jnp.float32
    )
    dq = (dq * (factor * SCALE)).astype(jnp.bfloat16)
    dq_send[c, strip] = dq.reshape(dq_send.shape[2:])
    parts = (
        jnp.dot(grad_logit, query, preferred_element_type=jnp.float32),
        jnp.dot(prob.astype(jnp.bfloat16), grad, preferred_element_type=jnp.float32),
    )
    for kind, part in enumerate(parts):
        if strip == 0:
            acc[slot, kind, :SPAN] = part
        else:
            acc[slot, kind, low : low + WINDOW] += part[:WINDOW]
            acc[slot, kind, low + WINDOW : low + SPAN] = part[WINDOW:]


def kernel(
    n, pairs, rows, q_ref, g_ref, k_ref, v_ref, turn_ref, mask_ref,
    dq_ref, dk_ref, dv_ref,
    raw, kv_ref, ext, qq, gg, acc, bias, token, column, dq_send, dkv_send, far, far_in, near, near_in,
    mark_ref, marks, count, count_in,
    mark_send, mark_recv, count_send, count_recv, local_sem, own_sem, keep_sem,
    kv_send, kv_recv, q_send, q_recv, far_send, far_recv, near_send, near_recv,
    dq_ssem, dq_rsem, dkv_ssem, dkv_rsem,
):
    heads, group = q_ref.shape[1:3]
    half = heads // 2
    plane = 2 * rows
    planes = n // 2
    strips = plane // STRIP
    me = lax.axis_index("ctx")
    x = me % 2
    p = me // 2
    up, down = p + 1 < planes, p >= 1
    mine, theirs = x * half, (1 - x) * half
    bits = [("ctx", 1 << b) for b in range(n.bit_length() - 1)]
    bits += [("dp", 1 << b) for b in range(pairs.bit_length() - 1)]
    across, above, below = {"ctx": me + 1 - 2 * x}, {"ctx": me + 2}, {"ctx": me - 2}

    def remote(src, dst, send, recv, device):
        return pltpu.make_async_remote_copy(
            src_ref=src, dst_ref=dst, send_sem=send, recv_sem=recv,
            device_id=device, device_id_type=pl.DeviceIdType.MESH,
        )

    def partner(axis, bit):
        at = lax.axis_index(axis)
        return {axis: at + bit - 2 * bit * ((at // bit) % 2)}

    def place(c, hop, side, kind):
        return ext.at[c, kind, pl.ds((2 - hop) * plane + side * rows, rows), :]

    def kv_copy(what, src, dst, c, kind, device):
        return remote(src, dst, kv_send.at[what, c, kind], kv_recv.at[what, c, kind], device)

    def kv_across(c, kind):
        return kv_copy(0, kv_ref.at[theirs + c, kind], place(c, 0, x, kind), c, kind, across)

    def own_up(c, kind):
        return kv_copy(1, kv_ref.at[mine + c, kind], place(c, 1, x, kind), c, kind, above)

    def other_up(c, kind):
        return kv_copy(2, place(c, 0, 1 - x, kind), place(c, 1, 1 - x, kind), c, kind, above)

    def own_on(c, kind):
        return kv_copy(3, place(c, 1, x, kind), place(c, 2, x, kind), c, kind, above)

    def other_on(c, kind):
        return kv_copy(4, place(c, 1, 1 - x, kind), place(c, 2, 1 - x, kind), c, kind, above)

    def q_across(c):
        return remote(q_ref.at[:, theirs + c], qq.at[c, x],
                      q_send.at[0, c], q_recv.at[0, c], across)

    def g_across(c):
        return remote(g_ref.at[:, theirs + c], gg.at[c, x],
                      q_send.at[1, c], q_recv.at[1, c], across)

    def far_copy(c, s):
        return remote(far.at[c, s], far_in.at[c, s], far_send.at[c, s], far_recv.at[c, s], below)

    def near_copy(c, s):
        return remote(near.at[c, s], near_in.at[c, s], near_send.at[c, s], near_recv.at[c, s],
                      below)

    def dq_copy(c, i):
        return remote(dq_send.at[c, 2 * (1 - x) + i],
                      dq_ref.at[pl.ds(i * STRIP, STRIP), mine + c],
                      dq_ssem.at[c, i], dq_rsem.at[c, i], across)

    def dq_keep(c, i):
        return pltpu.make_async_copy(dq_send.at[c, 2 * x + i],
                                     dq_ref.at[pl.ds(i * STRIP, STRIP), mine + c],
                                     keep_sem.at[c, i])

    def dkv_copy(c, i, kind):
        return remote(dkv_send.at[c, 2 * (1 - x) + i, kind],
                      (dk_ref, dv_ref)[kind].at[mine + c, pl.ds(i * STRIP, STRIP), :],
                      dkv_ssem.at[c, i, kind], dkv_rsem.at[c, i, kind], across)

    def count_copy(k):
        return remote(count.at[k], count_in.at[k], count_send.at[k], count_recv.at[k],
                      partner(*bits[k]))

    def mark_copy(hop, side):
        k = 2 * hop + side
        return remote(mark_ref, marks.at[2 * hop + x], mark_send.at[k], mark_recv.at[2 * hop + x],
                      {"ctx": 2 * (p + hop) + side})

    def mark_arrival(hop, side):
        k = 2 * hop + side
        return remote(mark_ref, marks.at[k], mark_send.at[k], mark_recv.at[k],
                      {"ctx": 2 * (p + hop) + side})

    raw_copies = [
        pltpu.make_async_copy(ref, raw.at[kind], local_sem.at[kind])
        for kind, ref in enumerate((k_ref, v_ref))
    ]
    own = [
        pltpu.make_async_copy(ref.at[:, mine + c], buffer.at[c, x], own_sem.at[kind, c])
        for c in range(half)
        for kind, (ref, buffer) in enumerate(((q_ref, qq), (g_ref, gg)))
    ]
    for copy in raw_copies:
        copy.start()
    barrier = pltpu.get_barrier_semaphore()

    def greet(device):
        pl.semaphore_signal(barrier, inc=1, device_id=device,
                            device_id_type=pl.DeviceIdType.MESH)

    greet(across)
    for hop in (1, 2):
        for side in (0, 1):
            @pl.when(p + hop < planes)
            def _():
                greet({"ctx": 2 * (p + hop) + side})

            @pl.when(p >= hop)
            def _():
                greet({"ctx": 2 * (p - hop) + side})
    distant = [b for b in bits if b[0] == "dp" or b[1] > 4]
    for b in distant:
        greet(partner(*b))
    for copy in own:
        copy.start()
    for kind, copy in enumerate(raw_copies):
        copy.wait()
        kv_ref[:, kind] = jnp.swapaxes(raw[kind], 0, 1)
    pl.semaphore_wait(
        barrier,
        1 + 2 * jnp.minimum(p, 2) + 2 * jnp.minimum(planes - 1 - p, 2) + len(distant),
    )

    def give(c):
        for kind in (0, 1):
            kv_across(c, kind).start()

    def give_q(c):
        q_across(c).start()
        g_across(c).start()

    def send_own(c):
        @pl.when(up)
        def _():
            for kind in (0, 1):
                own_up(c, kind).start()

    def pass_up(c):
        for kind in (0, 1):
            kv_across(c, kind).wait_recv()

            @pl.when(up)
            def _():
                other_up(c, kind).start()

    def pass_on(copy_in, copy_on, c):
        @pl.when(down)
        def _():
            for kind in (0, 1):
                copy_in(c, kind).wait_recv()

                @pl.when(up)
                def _():
                    copy_on(c, kind).start()

    give(0)
    send_own(0)
    line = lax.broadcasted_iota(jnp.int32, mark_ref.shape, 0)
    mark_ref[...] = jnp.where(line == 0, turn_ref[...], mask_ref[...])
    for side in (0, 1):
        @pl.when(x != side)
        def _():
            mark_copy(0, side).start()
    for hop in (1, 2):
        for side in (0, 1):
            @pl.when(p + hop < planes)
            def _():
                mark_copy(hop, side).start()
    ones = jnp.sum(mask_ref[...].astype(jnp.float32), axis=1, keepdims=True)
    count[0] = jnp.broadcast_to(ones, count.shape[1:])
    count_copy(0).start()
    for c in range(1, half):
        give(c)
        give_q(c - 1)
    give_q(half - 1)

    own_place = pltpu.make_async_copy(
        kv_ref.at[pl.ds(mine, half)],
        ext.at[:, :, pl.ds(2 * plane + x * rows, rows), :],
        local_sem.at[2],
    )
    own_place.start()

    for hop in (1, 2):
        @pl.when(p < hop)
        def _():
            def clear(c, carry):
                ext[c, :, (2 - hop) * plane : (3 - hop) * plane, :] = jnp.zeros(
                    (2, plane, ext.shape[3]), ext.dtype
                )
                return carry

            lax.fori_loop(0, half, clear, 0)

    def counted(k):
        count_copy(k).wait_recv()
        count[k + 1] = count[k] + count_in[k]
        if k + 1 < len(bits):
            count_copy(k + 1).start()

    def marks_here(hop):
        for side in (0, 1):
            at = ((2 - hop) * plane + side * rows) // STRIP * STRIP
            k = 2 * hop + side

            def lay(source):
                for part in range(rows // STRIP):
                    line = source[part * STRIP : (part + 1) * STRIP]
                    column[at + part * STRIP : at + (part + 1) * STRIP, :] = jnp.transpose(
                        jnp.broadcast_to(line[None], (STRIP, STRIP))
                    )

            present = (x != side) if hop == 0 else (p >= hop)

            @pl.when(present)
            def _():
                mark_arrival(hop, side).wait_recv()
                lay(marks[k, 0].astype(jnp.float32))

            @pl.when(jnp.logical_not(present))
            def _():
                if hop == 0:
                    marks[k] = mark_ref[...]
                    lay(mark_ref[0].astype(jnp.float32))
                else:
                    column[at : at + rows, :] = jnp.full((rows, STRIP), -1.0, jnp.float32)

    shift = group.bit_length() - 1

    def fill_bias(strip):
        low = strip * STRIP
        lines = marks[low // rows, :, low % rows : low % rows + STRIP]
        wide = (STRIP, STRIP * group)
        spread = (
            lax.broadcasted_iota(jnp.int32, wide, 1) >> shift
        ) == lax.broadcasted_iota(jnp.int32, wide, 0)
        token[strip] = jnp.dot(
            lines.astype(jnp.float32).astype(jnp.bfloat16),
            jnp.where(spread, 1.0, 0.0).astype(jnp.bfloat16),
            preferred_element_type=jnp.float32,
        )
        shape = (SPAN, STRIP * group)
        row = lax.broadcasted_iota(jnp.int32, shape, 1) >> shift
        col = lax.broadcasted_iota(jnp.int32, shape, 0)
        turn = jnp.concatenate([column[low : low + SPAN, :]] * group, axis=1)
        ok = (turn == token[strip, 0:1, :]) & (col > row) & (col <= row + WINDOW)
        bias[strip] = jnp.where(ok, 0.0, MASKED)

    pass_up(0)
    counted(0)
    for hop in (0, 1, 2):
        marks_here(hop)
    fill_bias(0)
    counted(1)
    fill_bias(1)
    pass_on(own_up, own_on, 0)
    fill_bias(2)
    fill_bias(3)
    for k in range(2, len(bits)):
        counted(k)
    pass_on(other_up, other_on, 0)
    send_own(1)
    pass_up(1)
    for copy in own:
        copy.wait()
    own_place.wait()

    factor = (rows * n * pairs) / count[len(bits), 0:1, 0:1]

    def pass_back(c):
        @pl.when(down)
        def _():
            for s in range(strips):
                at = plane + s * STRIP

                @pl.when(up)
                def _():
                    far_copy(c, s).wait_recv()
                    near[c, s] = (
                        acc[c % 2, :, at : at + STRIP, :] + far_in[c, s].astype(jnp.float32)
                    ).astype(near.dtype)

                @pl.when(jnp.logical_not(up))
                def _():
                    near[c, s] = acc[c % 2, :, at : at + STRIP, :].astype(near.dtype)

                near_copy(c, s).start()

    def finish(c):
        for s in range(strips):
            side, i = s // 2, s % 2
            at = 2 * plane + s * STRIP

            @pl.when(up)
            def _():
                near_copy(c, s).wait_recv()
                acc[c % 2, :, at : at + STRIP, :] += near_in[c, s].astype(jnp.float32)

            for kind, out in enumerate((dk_ref, dv_ref)):
                scale = factor * SCALE if kind == 0 else factor
                dkv_send[c, s, kind] = (
                    acc[c % 2, kind, at : at + STRIP, :] * scale
                ).astype(dkv_send.dtype)

                @pl.when(x == side)
                def _():
                    out[mine + c, i * STRIP : (i + 1) * STRIP, :] = dkv_send[c, s, kind]

                @pl.when(x != side)
                def _():
                    dkv_copy(c, i, kind).start()

    def step(c, carry):
        @pl.when(c >= 1)
        def _():
            pass_back(c - 1)

        q_across(c).wait_recv()
        g_across(c).wait_recv()

        @pl.when(p >= 2)
        def _():
            for kind in (0, 1):
                own_on(c, kind).wait_recv()
                other_on(c, kind).wait_recv()

        for s in range(strips):
            strip_grads(c, s, c % 2, qq, gg, ext, bias, token, acc, factor, dq_send)
            side, i = s // 2, s % 2

            @pl.when(p >= 2)
            def _():
                far[c, s] = acc[c % 2, :, s * STRIP : (s + 1) * STRIP, :].astype(far.dtype)
                far_copy(c, s).start()

            @pl.when(x == side)
            def _():
                dq_keep(c, i).start()

            @pl.when(x != side)
            def _():
                dq_copy(c, i).start()

            if s == 1:
                @pl.when(c + 1 < half)
                def _():
                    pass_on(own_up, own_on, c + 1)

        @pl.when(c + 1 < half)
        def _():
            pass_on(other_up, other_on, c + 1)

        @pl.when(c + 2 < half)
        def _():
            send_own(c + 2)
            pass_up(c + 2)

        @pl.when(c >= 1)
        def _():
            finish(c - 1)

        return carry

    lax.fori_loop(0, half, step, 0)
    pass_back(half - 1)
    finish(half - 1)

    def drain(c, carry):
        q_across(c).wait_send()
        g_across(c).wait_send()
        for i in range(2):
            dq_keep(c, i).wait()
            dq_copy(c, i).wait()
            for kind in (0, 1):
                dkv_copy(c, i, kind).wait()
        for kind in (0, 1):
            kv_across(c, kind).wait_send()

            @pl.when(up)
            def _():
                own_up(c, kind).wait_send()
                other_up(c, kind).wait_send()

                @pl.when(down)
                def _():
                    own_on(c, kind).wait_send()
                    other_on(c, kind).wait_send()

        for s in range(strips):
            @pl.when(down)
            def _():
                near_copy(c, s).wait_send()

            @pl.when(p >= 2)
            def _():
                far_copy(c, s).wait_send()
        return carry

    lax.fori_loop(0, half, drain, 0)
    for side in (0, 1):
        @pl.when(x != side)
        def _():
            mark_copy(0, side).wait_send()
    for hop in (1, 2):
        for side in (0, 1):
            @pl.when(p + hop < planes)
            def _():
                mark_copy(hop, side).wait_send()
    for k in range(len(bits)):
        count_copy(k).wait_send()


def place_outputs(dq_in, dk_in, dv_in, dq_out, dk_out, dv_out, held, before, after, sem, out_sem):
    parts = sem.shape[0] - 2
    part = dq_in.shape[0] // parts
    copy = pltpu.make_async_copy
    cuts = [pl.ds(k * part, part) for k in range(parts)]
    loads = [copy(ref, before.at[k], sem.at[k]) for k, ref in enumerate((dk_in, dv_in))]
    loads += [copy(dq_in.at[cut], held.at[cut], sem.at[2 + k]) for k, cut in enumerate(cuts)]
    stores = [copy(after.at[k], ref, out_sem.at[k]) for k, ref in enumerate((dk_out, dv_out))]
    stores += [copy(held.at[cut], dq_out.at[cut], out_sem.at[2 + k]) for k, cut in enumerate(cuts)]
    for load in loads:
        load.start()
    for k in range(2 + parts):
        loads[k].wait()
        if k < 2:
            after[k] = jnp.swapaxes(before[k], 0, 1)
        stores[k].start()
    for store in stores:
        store.wait()


def on_device(queries, keys, values, d_out, loss_mask, turn_ids):
    rows, heads_q, depth = queries.shape[1:]
    heads = keys.shape[2]
    half = heads // 2
    group = heads_q // heads
    n = lax.axis_size("ctx")
    plane = 2 * rows
    strips = rows // STRIP
    wide = group * STRIP
    pairs = lax.axis_size("dp")
    rounds = n.bit_length() + pairs.bit_length() - 2

    def by_group(array):
        return array.reshape(rows, heads, group, depth)

    vmem = pl.BlockSpec(memory_space=pltpu.VMEM)
    anywhere = pl.BlockSpec(memory_space=pl.ANY)
    bf16, f32 = jnp.bfloat16, jnp.float32
    dma = pltpu.SemaphoreType.DMA
    dq, dk, dv = pl.pallas_call(
        functools.partial(kernel, n, pairs, rows),
        out_shape=(
            jax.ShapeDtypeStruct((rows, heads, group, depth), bf16),
            jax.ShapeDtypeStruct((heads, rows, depth), bf16),
            jax.ShapeDtypeStruct((heads, rows, depth), bf16),
        ),
        in_specs=[anywhere] * 4 + [vmem] * 2,
        out_specs=(anywhere, vmem, vmem),
        scratch_shapes=[
            pltpu.VMEM((2, rows, heads, depth), bf16),
            pltpu.VMEM((heads, 2, rows, depth), bf16),
            pltpu.VMEM((half, 2, WINDOW + plane, depth), bf16),
            pltpu.VMEM((half, 2, rows, group, depth), bf16),
            pltpu.VMEM((half, 2, rows, group, depth), bf16),
            pltpu.VMEM((2, 2, WINDOW + plane, depth), f32),
            pltpu.VMEM((2 * strips, SPAN, wide), f32),
            pltpu.VMEM((2 * strips, 8, wide), f32),
            pltpu.VMEM((WINDOW + plane, STRIP), f32),
            pltpu.VMEM((half, 2 * strips, STRIP, group, depth), bf16),
            pltpu.VMEM((half, 2 * strips, 2, STRIP, depth), bf16),
            pltpu.VMEM((half, 2 * strips, 2, STRIP, depth), bf16),
            pltpu.VMEM((half, 2 * strips, 2, STRIP, depth), bf16),
            pltpu.VMEM((half, 2 * strips, 2, STRIP, depth), bf16),
            pltpu.VMEM((half, 2 * strips, 2, STRIP, depth), bf16),
            pltpu.VMEM((8, rows), jnp.int32),
            pltpu.VMEM((6, 8, rows), jnp.int32),
            pltpu.VMEM((rounds + 1, 8, 128), f32),
            pltpu.VMEM((rounds, 8, 128), f32),
            dma((6,)),
            dma((6,)),
            dma((rounds,)),
            dma((rounds,)),
            dma((3,)),
            dma((2, half)),
            dma((half, strips)),
            dma((5, half, 2)),
            dma((5, half, 2)),
            dma((2, half)),
            dma((2, half)),
            dma((half, 2 * strips)),
            dma((half, 2 * strips)),
            dma((half, 2 * strips)),
            dma((half, 2 * strips)),
            dma((half, strips)),
            dma((half, strips)),
            dma((half, strips, 2)),
            dma((half, strips, 2)),
        ],
        compiler_params=pltpu.CompilerParams(
            collective_id=0, has_side_effects=True, vmem_limit_bytes=56 << 20
        ),
    )(by_group(queries[0]), by_group(d_out[0]), keys[0], values[0], turn_ids, loss_mask)
    dq, dk, dv = pl.pallas_call(
        place_outputs,
        out_shape=(
            jax.ShapeDtypeStruct((rows, heads, group, depth), bf16),
            jax.ShapeDtypeStruct((rows, heads, depth), bf16),
            jax.ShapeDtypeStruct((rows, heads, depth), bf16),
        ),
        in_specs=[anywhere] * 3,
        out_specs=(anywhere,) * 3,
        scratch_shapes=[
            pltpu.VMEM((rows, heads, group, depth), bf16),
            pltpu.VMEM((2, heads, rows, depth), bf16),
            pltpu.VMEM((2, rows, heads, depth), bf16),
            dma((6,)),
            dma((6,)),
        ],
    )(dq, dk, dv)
    return (dq.reshape(1, rows, heads_q, depth), dk[None], dv[None])


def solution(mesh):
    spec = P("dp", "ctx", "head", None)
    return jax.shard_map(
        on_device,
        mesh=mesh,
        in_specs=(spec, spec, spec, spec, P("dp", "ctx"), P("dp", "ctx")),
        out_specs=(spec, spec, spec),
        check_vma=False,
    )
```

```python
import functools
import math

import jax
import jax.numpy as jnp
from jax import lax
from jax.experimental import pallas as pl
from jax.experimental.pallas import tpu as pltpu
from jax.sharding import PartitionSpec as P

WINDOW = 1024
SCALE = 168.0 ** (-0.5)
STRIP = 128
SPAN = WINDOW + STRIP
MASKED = -1e30


def strip_grads(c, strip, slot, qq, gg, ext, bias, token, acc, factor, dq_send):
    low = strip * STRIP
    side, i = low // qq.shape[2], low % qq.shape[2]
    wide = (STRIP * qq.shape[3], qq.shape[4])
    query = qq[c, side, i : i + STRIP].reshape(wide)
    grad = gg[c, side, i : i + STRIP].reshape(wide)
    key = ext[c, 0, low : low + SPAN, :]
    value = ext[c, 1, low : low + SPAN, :]
    logits = lax.dot_general(
        key, query, (((1,), (1,)), ((), ())), preferred_element_type=jnp.float32
    )
    logits = logits * (SCALE * math.log2(math.e)) + bias[strip]
    top = jnp.max(logits, axis=0, keepdims=True)
    raised = jnp.exp2(logits - top)
    prob = raised * (token[strip, 1:2, :] / jnp.sum(raised, axis=0, keepdims=True))
    grad_prob = lax.dot_general(
        value, grad, (((1,), (1,)), ((), ())), preferred_element_type=jnp.float32
    )
    delta = jnp.sum(prob * grad_prob, axis=0, keepdims=True)
    grad_logit = (prob * (grad_prob - delta)).astype(jnp.bfloat16)
    dq = lax.dot_general(
        grad_logit, key, (((0,), (0,)), ((), ())), preferred_element_type=jnp.float32
    )
    dq = (dq * (factor * SCALE)).astype(jnp.bfloat16)
    dq_send[c, strip] = dq.reshape(dq_send.shape[2:])
    parts = (
        jnp.dot(grad_logit, query, preferred_element_type=jnp.float32),
        jnp.dot(prob.astype(jnp.bfloat16), grad, preferred_element_type=jnp.float32),
    )
    for kind, part in enumerate(parts):
        if strip == 0:
            acc[slot, kind, :SPAN] = part
        else:
            acc[slot, kind, low : low + WINDOW] += part[:WINDOW]
            acc[slot, kind, low + WINDOW : low + SPAN] = part[WINDOW:]


def kernel(
    n, pairs, rows, q_ref, g_ref, k_ref, v_ref, turn_ref, mask_ref,
    dq_ref, dk_ref, dv_ref,
    raw, kv_ref, ext, qq, gg, acc, bias, token, column, dq_send, dkv_send, far, far_in, near, near_in, part, part_in, cross_in,
    mark_ref, marks, count, count_in,
    mark_send, mark_recv, count_send, count_recv, local_sem, own_sem, keep_sem,
    kv_send, kv_recv, q_send, q_recv, far_send, far_recv, near_send, near_recv,
    dq_ssem, dq_rsem, dkv_ssem, dkv_rsem, part_send, part_recv, cross_recv,
):
    heads, group = q_ref.shape[1:3]
    half = heads // 2
    plane = 2 * rows
    planes = n // 2
    strips = plane // STRIP
    me = lax.axis_index("ctx")
    x = me % 2
    p = me // 2
    up, down = p + 1 < planes, p >= 1
    mine, theirs = x * half, (1 - x) * half
    bits = [("ctx", 1 << b) for b in range(n.bit_length() - 1)]
    bits += [("dp", 1 << b) for b in range(pairs.bit_length() - 1)]
    across, above, below = {"ctx": me + 1 - 2 * x}, {"ctx": me + 2}, {"ctx": me - 2}

    def remote(src, dst, send, recv, device):
        return pltpu.make_async_remote_copy(
            src_ref=src, dst_ref=dst, send_sem=send, recv_sem=recv,
            device_id=device, device_id_type=pl.DeviceIdType.MESH,
        )

    def partner(axis, bit):
        at = lax.axis_index(axis)
        return {axis: at + bit - 2 * bit * ((at // bit) % 2)}

    def place(c, hop, side, kind):
        return ext.at[c, kind, pl.ds((2 - hop) * plane + side * rows, rows), :]

    def kv_copy(what, src, dst, c, kind, device):
        return remote(src, dst, kv_send.at[what, c, kind], kv_recv.at[what, c, kind], device)

    def kv_across(c, kind):
        return kv_copy(0, kv_ref.at[theirs + c, kind], place(c, 0, x, kind), c, kind, across)

    def own_up(c, kind):
        return kv_copy(1, kv_ref.at[mine + c, kind], place(c, 1, x, kind), c, kind, above)

    def other_up(c, kind):
        return kv_copy(2, place(c, 0, 1 - x, kind), place(c, 1, 1 - x, kind), c, kind, above)

    def cross_up(c, kind):
        return kv_copy(2, kv_ref.at[theirs + c, kind], place(c, 1, x, kind), c, kind,
                       {"ctx": 2 * (p + 1) + 1 - x})

    def own_on(c, kind):
        return kv_copy(3, place(c, 1, x, kind), place(c, 2, x, kind), c, kind, above)

    def other_on(c, kind):
        return kv_copy(4, place(c, 1, 1 - x, kind), place(c, 2, 1 - x, kind), c, kind, above)

    def q_across(c):
        return remote(q_ref.at[:, theirs + c], qq.at[c, x],
                      q_send.at[0, c], q_recv.at[0, c], across)

    def g_across(c):
        return remote(g_ref.at[:, theirs + c], gg.at[c, x],
                      q_send.at[1, c], q_recv.at[1, c], across)

    def far_copy(c, s):
        return remote(far.at[c, s], far_in.at[c, s], far_send.at[c, s], far_recv.at[c, s], below)

    def near_copy(c, s):
        return remote(near.at[c, s], near_in.at[c, s], near_send.at[c, s], near_recv.at[c, s],
                      below)

    last = half - 1

    def near_cross(i, s):
        return remote(near.at[last, s], cross_in.at[i], near_send.at[last, s], cross_recv.at[i],
                      {"ctx": 2 * (p - 1) + 1 - x})

    def part_copy(i):
        return remote(part.at[i], part_in.at[i], part_send.at[i], part_recv.at[i], across)

    def dq_copy(c, i):
        return remote(dq_send.at[c, 2 * (1 - x) + i],
                      dq_ref.at[pl.ds(i * STRIP, STRIP), mine + c],
                      dq_ssem.at[c, i], dq_rsem.at[c, i], across)

    def dq_keep(c, i):
        return pltpu.make_async_copy(dq_send.at[c, 2 * x + i],
                                     dq_ref.at[pl.ds(i * STRIP, STRIP), mine + c],
                                     keep_sem.at[c, i])

    def dkv_copy(c, i, kind):
        return remote(dkv_send.at[c, 2 * (1 - x) + i, kind],
                      (dk_ref, dv_ref)[kind].at[mine + c, pl.ds(i * STRIP, STRIP), :],
                      dkv_ssem.at[c, i, kind], dkv_rsem.at[c, i, kind], across)

    def count_copy(k):
        return remote(count.at[k], count_in.at[k], count_send.at[k], count_recv.at[k],
                      partner(*bits[k]))

    def mark_copy(hop, side):
        k = 2 * hop + side
        return remote(mark_ref, marks.at[2 * hop + x], mark_send.at[k], mark_recv.at[2 * hop + x],
                      {"ctx": 2 * (p + hop) + side})

    def mark_arrival(hop, side):
        k = 2 * hop + side
        return remote(mark_ref, marks.at[k], mark_send.at[k], mark_recv.at[k],
                      {"ctx": 2 * (p + hop) + side})

    raw_copies = [
        pltpu.make_async_copy(ref, raw.at[kind], local_sem.at[kind])
        for kind, ref in enumerate((k_ref, v_ref))
    ]
    own = [
        pltpu.make_async_copy(ref.at[:, mine + c], buffer.at[c, x], own_sem.at[kind, c])
        for c in range(half)
        for kind, (ref, buffer) in enumerate(((q_ref, qq), (g_ref, gg)))
    ]
    for copy in raw_copies:
        copy.start()
    barrier = pltpu.get_barrier_semaphore()

    def greet(device):
        pl.semaphore_signal(barrier, inc=1, device_id=device,
                            device_id_type=pl.DeviceIdType.MESH)

    greet(across)
    for hop in (1, 2):
        for side in (0, 1):
            @pl.when(p + hop < planes)
            def _():
                greet({"ctx": 2 * (p + hop) + side})

            @pl.when(p >= hop)
            def _():
                greet({"ctx": 2 * (p - hop) + side})
    distant = [b for b in bits if b[0] == "dp" or b[1] > 4]
    for b in distant:
        greet(partner(*b))
    for copy in own:
        copy.start()
    for kind, copy in enumerate(raw_copies):
        copy.wait()
        kv_ref[:, kind] = jnp.swapaxes(raw[kind], 0, 1)
    pl.semaphore_wait(
        barrier,
        1 + 2 * jnp.minimum(p, 2) + 2 * jnp.minimum(planes - 1 - p, 2) + len(distant),
    )

    def give(c):
        for kind in (0, 1):
            kv_across(c, kind).start()

    def give_q(c):
        q_across(c).start()
        g_across(c).start()

    def send_own(c):
        @pl.when(up)
        def _():
            for kind in (0, 1):
                own_up(c, kind).start()

    def pass_up(c):
        for kind in (0, 1):
            kv_across(c, kind).wait_recv()

            @pl.when(up)
            def _():
                other_up(c, kind).start()

    def pass_on(copy_in, copy_on, c):
        @pl.when(down)
        def _():
            for kind in (0, 1):
                copy_in(c, kind).wait_recv()

                @pl.when(up)
                def _():
                    copy_on(c, kind).start()

    give(0)
    send_own(0)

    @pl.when(up)
    def _():
        for kind in (0, 1):
            cross_up(0, kind).start()

    line = lax.broadcasted_iota(jnp.int32, mark_ref.shape, 0)
    mark_ref[...] = jnp.where(line == 0, turn_ref[...], mask_ref[...])
    for side in (0, 1):
        @pl.when(x != side)
        def _():
            mark_copy(0, side).start()
    for hop in (1, 2):
        for side in (0, 1):
            @pl.when(p + hop < planes)
            def _():
                mark_copy(hop, side).start()
    ones = jnp.sum(mask_ref[...].astype(jnp.float32), axis=1, keepdims=True)
    count[0] = jnp.broadcast_to(ones, count.shape[1:])
    count_copy(0).start()
    for c in range(1, half):
        give(c)
        give_q(c - 1)
    give_q(half - 1)

    own_place = pltpu.make_async_copy(
        kv_ref.at[pl.ds(mine, half)],
        ext.at[:, :, pl.ds(2 * plane + x * rows, rows), :],
        local_sem.at[2],
    )
    own_place.start()

    for hop in (1, 2):
        @pl.when(p < hop)
        def _():
            def clear(c, carry):
                ext[c, :, (2 - hop) * plane : (3 - hop) * plane, :] = jnp.zeros(
                    (2, plane, ext.shape[3]), ext.dtype
                )
                return carry

            lax.fori_loop(0, half, clear, 0)

    def counted(k):
        count_copy(k).wait_recv()
        count[k + 1] = count[k] + count_in[k]
        if k + 1 < len(bits):
            count_copy(k + 1).start()

    def marks_here(hop):
        for side in (0, 1):
            at = ((2 - hop) * plane + side * rows) // STRIP * STRIP
            k = 2 * hop + side

            def lay(source):
                for part in range(rows // STRIP):
                    line = source[part * STRIP : (part + 1) * STRIP]
                    column[at + part * STRIP : at + (part + 1) * STRIP, :] = jnp.transpose(
                        jnp.broadcast_to(line[None], (STRIP, STRIP))
                    )

            present = (x != side) if hop == 0 else (p >= hop)

            @pl.when(present)
            def _():
                mark_arrival(hop, side).wait_recv()
                lay(marks[k, 0].astype(jnp.float32))

            @pl.when(jnp.logical_not(present))
            def _():
                if hop == 0:
                    marks[k] = mark_ref[...]
                    lay(mark_ref[0].astype(jnp.float32))
                else:
                    column[at : at + rows, :] = jnp.full((rows, STRIP), -1.0, jnp.float32)

    shift = group.bit_length() - 1

    def fill_bias(strip):
        low = strip * STRIP
        lines = marks[low // rows, :, low % rows : low % rows + STRIP]
        wide = (STRIP, STRIP * group)
        spread = (
            lax.broadcasted_iota(jnp.int32, wide, 1) >> shift
        ) == lax.broadcasted_iota(jnp.int32, wide, 0)
        token[strip] = jnp.dot(
            lines.astype(jnp.float32).astype(jnp.bfloat16),
            jnp.where(spread, 1.0, 0.0).astype(jnp.bfloat16),
            preferred_element_type=jnp.float32,
        )
        shape = (SPAN, STRIP * group)
        row = lax.broadcasted_iota(jnp.int32, shape, 1) >> shift
        col = lax.broadcasted_iota(jnp.int32, shape, 0)
        turn = jnp.concatenate([column[low : low + SPAN, :]] * group, axis=1)
        ok = (turn == token[strip, 0:1, :]) & (col > row) & (col <= row + WINDOW)
        bias[strip] = jnp.where(ok, 0.0, MASKED)

    counted(0)
    for hop in (0, 1, 2):
        marks_here(hop)
    pass_on(own_up, own_on, 0)
    counted(1)
    fill_bias(0)
    pass_on(other_up, other_on, 0)
    send_own(1)
    pass_up(1)
    counted(2)
    fill_bias(1)
    fill_bias(2)
    fill_bias(3)
    for kind in (0, 1):
        kv_across(0, kind).wait_recv()
    for k in range(3, len(bits)):
        counted(k)
    for copy in own:
        copy.wait()
    own_place.wait()

    factor = (rows * n * pairs) / count[len(bits), 0:1, 0:1]

    def pass_back(c):
        @pl.when(down)
        def _():
            for s in range(strips):
                at = plane + s * STRIP

                @pl.when(up)
                def _():
                    far_copy(c, s).wait_recv()
                    near[c, s] = (
                        acc[c % 2, :, at : at + STRIP, :] + far_in[c, s].astype(jnp.float32)
                    ).astype(near.dtype)

                @pl.when(jnp.logical_not(up))
                def _():
                    near[c, s] = acc[c % 2, :, at : at + STRIP, :].astype(near.dtype)

                if isinstance(c, int):
                    @pl.when(x == s // 2)
                    def _():
                        near_copy(c, s).start()

                    @pl.when(x != s // 2)
                    def _():
                        near_cross(s % 2, s).start()
                else:
                    near_copy(c, s).start()

    def finish_last():
        slot = last % 2
        for i in range(rows // STRIP):
            at = pl.ds(2 * plane + x * rows + i * STRIP, STRIP)
            own_rows = slice(i * STRIP, (i + 1) * STRIP)

            @pl.when(up)
            def _():
                near_copy(last, 2 * x + i).wait_recv()
                acc[slot, :, at, :] += near_in[last, 2 * x + i].astype(jnp.float32)

            for kind, out in enumerate((dk_ref, dv_ref)):
                scale = factor * SCALE if kind == 0 else factor
                out[mine + last, own_rows, :] = (acc[slot, kind, at, :] * scale).astype(out.dtype)
        for i in range(rows // STRIP):
            own_rows = slice(i * STRIP, (i + 1) * STRIP)
            part_copy(i).wait_recv()

            def deliver(total):
                for kind, out in enumerate((dk_ref, dv_ref)):
                    scale = factor * SCALE if kind == 0 else factor
                    out[theirs + last, own_rows, :] = (total[kind] * scale).astype(out.dtype)

            @pl.when(up)
            def _():
                near_cross(i, 2 * x + i).wait_recv()
                deliver(part_in[i].astype(jnp.float32) + cross_in[i].astype(jnp.float32))

            @pl.when(jnp.logical_not(up))
            def _():
                deliver(part_in[i].astype(jnp.float32))

    def finish(c):
        for s in range(strips):
            side, i = s // 2, s % 2
            at = 2 * plane + s * STRIP

            @pl.when(up)
            def _():
                near_copy(c, s).wait_recv()
                acc[c % 2, :, at : at + STRIP, :] += near_in[c, s].astype(jnp.float32)

            for kind, out in enumerate((dk_ref, dv_ref)):
                scale = factor * SCALE if kind == 0 else factor
                dkv_send[c, s, kind] = (
                    acc[c % 2, kind, at : at + STRIP, :] * scale
                ).astype(dkv_send.dtype)

                @pl.when(x == side)
                def _():
                    out[mine + c, i * STRIP : (i + 1) * STRIP, :] = dkv_send[c, s, kind]

                @pl.when(x != side)
                def _():
                    dkv_copy(c, i, kind).start()

    def step(c, carry):
        @pl.when(c >= 1)
        def _():
            pass_back(c - 1)

        q_across(c).wait_recv()
        g_across(c).wait_recv()

        @pl.when(p >= 2)
        def _():
            for kind in (0, 1):
                own_on(c, kind).wait_recv()
                other_on(c, kind).wait_recv()

        for s in range(strips):
            if s == 3:
                @pl.when(c >= 1)
                def _():
                    finish(c - 1)

            strip_grads(c, s, c % 2, qq, gg, ext, bias, token, acc, factor, dq_send)
            side, i = s // 2, s % 2

            @pl.when(p >= 2)
            def _():
                far[c, s] = acc[c % 2, :, s * STRIP : (s + 1) * STRIP, :].astype(far.dtype)
                far_copy(c, s).start()

            @pl.when(x == side)
            def _():
                dq_keep(c, i).start()

            @pl.when(x != side)
            def _():
                dq_copy(c, i).start()

            if s == 1:
                @pl.when(c + 1 < half)
                def _():
                    pass_on(own_up, own_on, c + 1)

        @pl.when(c + 1 < half)
        def _():
            pass_on(other_up, other_on, c + 1)

        @pl.when(c + 2 < half)
        def _():
            send_own(c + 2)
            pass_up(c + 2)

        return carry

    lax.fori_loop(0, half, step, 0)
    for i in range(rows // STRIP):
        at = pl.ds(2 * plane + (1 - x) * rows + i * STRIP, STRIP)
        part[i] = acc[last % 2, :, at, :].astype(part.dtype)
        part_copy(i).start()
    pass_back(last)
    finish_last()

    def drain(c, carry):
        q_across(c).wait_send()
        g_across(c).wait_send()
        for i in range(2):
            dq_keep(c, i).wait()
            dq_copy(c, i).wait()

            @pl.when(c < last)
            def _():
                for kind in (0, 1):
                    dkv_copy(c, i, kind).wait()
        for kind in (0, 1):
            kv_across(c, kind).wait_send()

            @pl.when(up)
            def _():
                own_up(c, kind).wait_send()
                other_up(c, kind).wait_send()

                @pl.when(down)
                def _():
                    own_on(c, kind).wait_send()
                    other_on(c, kind).wait_send()

        for s in range(strips):
            @pl.when(down)
            def _():
                near_copy(c, s).wait_send()

            @pl.when(p >= 2)
            def _():
                far_copy(c, s).wait_send()
        return carry

    lax.fori_loop(0, half, drain, 0)
    for i in range(rows // STRIP):
        part_copy(i).wait_send()
    for side in (0, 1):
        @pl.when(x != side)
        def _():
            mark_copy(0, side).wait_send()
    for hop in (1, 2):
        for side in (0, 1):
            @pl.when(p + hop < planes)
            def _():
                mark_copy(hop, side).wait_send()
    for k in range(len(bits)):
        count_copy(k).wait_send()


def place_outputs(dq_in, dk_in, dv_in, dq_out, dk_out, dv_out, held, before, after, sem, out_sem):
    parts = sem.shape[0] - 2
    part = dq_in.shape[0] // parts
    copy = pltpu.make_async_copy
    cuts = [pl.ds(k * part, part) for k in range(parts)]
    loads = [copy(ref, before.at[k], sem.at[k]) for k, ref in enumerate((dk_in, dv_in))]
    loads += [copy(dq_in.at[cut], held.at[cut], sem.at[2 + k]) for k, cut in enumerate(cuts)]
    stores = [copy(after.at[k], ref, out_sem.at[k]) for k, ref in enumerate((dk_out, dv_out))]
    stores += [copy(held.at[cut], dq_out.at[cut], out_sem.at[2 + k]) for k, cut in enumerate(cuts)]
    for load in loads:
        load.start()
    for k in range(2 + parts):
        loads[k].wait()
        if k < 2:
            after[k] = jnp.swapaxes(before[k], 0, 1)
        stores[k].start()
    for store in stores:
        store.wait()


def on_device(queries, keys, values, d_out, loss_mask, turn_ids):
    rows, heads_q, depth = queries.shape[1:]
    heads = keys.shape[2]
    half = heads // 2
    group = heads_q // heads
    n = lax.axis_size("ctx")
    plane = 2 * rows
    strips = rows // STRIP
    wide = group * STRIP
    pairs = lax.axis_size("dp")
    rounds = n.bit_length() + pairs.bit_length() - 2

    def by_group(array):
        return array.reshape(rows, heads, group, depth)

    vmem = pl.BlockSpec(memory_space=pltpu.VMEM)
    anywhere = pl.BlockSpec(memory_space=pl.ANY)
    bf16, f32 = jnp.bfloat16, jnp.float32
    dma = pltpu.SemaphoreType.DMA
    dq, dk, dv = pl.pallas_call(
        functools.partial(kernel, n, pairs, rows),
        out_shape=(
            jax.ShapeDtypeStruct((rows, heads, group, depth), bf16),
            jax.ShapeDtypeStruct((heads, rows, depth), bf16),
            jax.ShapeDtypeStruct((heads, rows, depth), bf16),
        ),
        in_specs=[anywhere] * 4 + [vmem] * 2,
        out_specs=(anywhere, vmem, vmem),
        scratch_shapes=[
            pltpu.VMEM((2, rows, heads, depth), bf16),
            pltpu.VMEM((heads, 2, rows, depth), bf16),
            pltpu.VMEM((half, 2, WINDOW + plane, depth), bf16),
            pltpu.VMEM((half, 2, rows, group, depth), bf16),
            pltpu.VMEM((half, 2, rows, group, depth), bf16),
            pltpu.VMEM((2, 2, WINDOW + plane, depth), f32),
            pltpu.VMEM((2 * strips, SPAN, wide), f32),
            pltpu.VMEM((2 * strips, 8, wide), f32),
            pltpu.VMEM((WINDOW + plane, STRIP), f32),
            pltpu.VMEM((half, 2 * strips, STRIP, group, depth), bf16),
            pltpu.VMEM((half, 2 * strips, 2, STRIP, depth), bf16),
            pltpu.VMEM((half, 2 * strips, 2, STRIP, depth), bf16),
            pltpu.VMEM((half, 2 * strips, 2, STRIP, depth), bf16),
            pltpu.VMEM((half, 2 * strips, 2, STRIP, depth), bf16),
            pltpu.VMEM((half, 2 * strips, 2, STRIP, depth), bf16),
            pltpu.VMEM((strips, 2, STRIP, depth), bf16),
            pltpu.VMEM((strips, 2, STRIP, depth), bf16),
            pltpu.VMEM((strips, 2, STRIP, depth), bf16),
            pltpu.VMEM((8, rows), jnp.int32),
            pltpu.VMEM((6, 8, rows), jnp.int32),
            pltpu.VMEM((rounds + 1, 8, 128), f32),
            pltpu.VMEM((rounds, 8, 128), f32),
            dma((6,)),
            dma((6,)),
            dma((rounds,)),
            dma((rounds,)),
            dma((3,)),
            dma((2, half)),
            dma((half, strips)),
            dma((5, half, 2)),
            dma((5, half, 2)),
            dma((2, half)),
            dma((2, half)),
            dma((half, 2 * strips)),
            dma((half, 2 * strips)),
            dma((half, 2 * strips)),
            dma((half, 2 * strips)),
            dma((half, strips)),
            dma((half, strips)),
            dma((half, strips, 2)),
            dma((half, strips, 2)),
            dma((strips,)),
            dma((strips,)),
            dma((strips,)),
        ],
        compiler_params=pltpu.CompilerParams(
            collective_id=0, has_side_effects=True, vmem_limit_bytes=56 << 20
        ),
    )(by_group(queries[0]), by_group(d_out[0]), keys[0], values[0], turn_ids, loss_mask)
    dq, dk, dv = pl.pallas_call(
        place_outputs,
        out_shape=(
            jax.ShapeDtypeStruct((rows, heads, group, depth), bf16),
            jax.ShapeDtypeStruct((rows, heads, depth), bf16),
            jax.ShapeDtypeStruct((rows, heads, depth), bf16),
        ),
        in_specs=[anywhere] * 3,
        out_specs=(anywhere,) * 3,
        scratch_shapes=[
            pltpu.VMEM((rows, heads, group, depth), bf16),
            pltpu.VMEM((2, heads, rows, depth), bf16),
            pltpu.VMEM((2, rows, heads, depth), bf16),
            dma((6,)),
            dma((6,)),
        ],
    )(dq, dk, dv)
    return (dq.reshape(1, rows, heads_q, depth), dk[None], dv[None])


def solution(mesh):
    spec = P("dp", "ctx", "head", None)
    return jax.shard_map(
        on_device,
        mesh=mesh,
        in_specs=(spec, spec, spec, spec, P("dp", "ctx"), P("dp", "ctx")),
        out_specs=(spec, spec, spec),
        check_vma=False,
    )
```

```python
import functools
import math

import jax
import jax.numpy as jnp
from jax import lax
from jax.experimental import pallas as pl
from jax.experimental.pallas import tpu as pltpu
from jax.sharding import PartitionSpec as P

WINDOW = 1024
SCALE = 168.0 ** (-0.5)
STRIP = 128
SPAN = WINDOW + STRIP
MASKED = -1e30


def strip_grads(c, strip, slot, qq, gg, ext, bias, token, acc, factor, dq_send):
    low = strip * STRIP
    side, i = low // qq.shape[2], low % qq.shape[2]
    wide = (STRIP * qq.shape[3], qq.shape[4])
    query = qq[c, side, i : i + STRIP].reshape(wide)
    grad = gg[c, side, i : i + STRIP].reshape(wide)
    key = ext[c, 0, low : low + SPAN, :]
    value = ext[c, 1, low : low + SPAN, :]
    logits = lax.dot_general(
        key, query, (((1,), (1,)), ((), ())), preferred_element_type=jnp.float32
    )
    logits = logits * (SCALE * math.log2(math.e)) + bias[strip]
    top = jnp.max(logits, axis=0, keepdims=True)
    raised = jnp.exp2(logits - top)
    prob = raised * (token[strip, 1:2, :] / jnp.sum(raised, axis=0, keepdims=True))
    grad_prob = lax.dot_general(
        value, grad, (((1,), (1,)), ((), ())), preferred_element_type=jnp.float32
    )
    delta = jnp.sum(prob * grad_prob, axis=0, keepdims=True)
    grad_logit = (prob * (grad_prob - delta)).astype(jnp.bfloat16)
    dq = jnp.transpose(
        lax.dot_general(
            key, grad_logit, (((0,), (0,)), ((), ())), preferred_element_type=jnp.float32
        )
    )
    dq = (dq * (factor * SCALE)).astype(jnp.bfloat16)
    dq_send[c, strip] = dq.reshape(dq_send.shape[2:])
    parts = (
        jnp.dot(grad_logit, query, preferred_element_type=jnp.float32),
        jnp.dot(prob.astype(jnp.bfloat16), grad, preferred_element_type=jnp.float32),
    )
    for kind, part in enumerate(parts):
        if strip == 0:
            acc[slot, kind, :SPAN] = part
        else:
            acc[slot, kind, low : low + WINDOW] += part[:WINDOW]
            acc[slot, kind, low + WINDOW : low + SPAN] = part[WINDOW:]


def kernel(
    n, pairs, rows, q_ref, g_ref, k_ref, v_ref, turn_ref, mask_ref,
    dq_ref, dk_ref, dv_ref,
    raw, kv_ref, ext, qq, gg, acc, bias, token, column, dq_send, dkv_send, far, far_in, near, near_in, part, part_in, cross_in,
    mark_ref, marks, count, count_in,
    mark_send, mark_recv, count_send, count_recv, local_sem, own_sem, keep_sem,
    kv_send, kv_recv, q_send, q_recv, far_send, far_recv, near_send, near_recv,
    dq_ssem, dq_rsem, dkv_ssem, dkv_rsem, part_send, part_recv, cross_recv,
):
    heads, group = q_ref.shape[1:3]
    half = heads // 2
    plane = 2 * rows
    planes = n // 2
    strips = plane // STRIP
    me = lax.axis_index("ctx")
    x = me % 2
    p = me // 2
    up, down = p + 1 < planes, p >= 1
    mine, theirs = x * half, (1 - x) * half
    bits = [("ctx", 1 << b) for b in range(n.bit_length() - 1)]
    bits += [("dp", 1 << b) for b in range(pairs.bit_length() - 1)]
    across, above, below = {"ctx": me + 1 - 2 * x}, {"ctx": me + 2}, {"ctx": me - 2}

    def remote(src, dst, send, recv, device):
        return pltpu.make_async_remote_copy(
            src_ref=src, dst_ref=dst, send_sem=send, recv_sem=recv,
            device_id=device, device_id_type=pl.DeviceIdType.MESH,
        )

    def partner(axis, bit):
        at = lax.axis_index(axis)
        return {axis: at + bit - 2 * bit * ((at // bit) % 2)}

    def place(c, hop, side, kind):
        return ext.at[c, kind, pl.ds((2 - hop) * plane + side * rows, rows), :]

    def kv_copy(what, src, dst, c, kind, device):
        return remote(src, dst, kv_send.at[what, c, kind], kv_recv.at[what, c, kind], device)

    def kv_across(c, kind):
        return kv_copy(0, kv_ref.at[theirs + c, kind], place(c, 0, x, kind), c, kind, across)

    def own_up(c, kind):
        return kv_copy(1, kv_ref.at[mine + c, kind], place(c, 1, x, kind), c, kind, above)

    def other_up(c, kind):
        return kv_copy(2, place(c, 0, 1 - x, kind), place(c, 1, 1 - x, kind), c, kind, above)

    def cross_up(c, kind):
        return kv_copy(2, kv_ref.at[theirs + c, kind], place(c, 1, x, kind), c, kind,
                       {"ctx": 2 * (p + 1) + 1 - x})

    def own_on(c, kind):
        return kv_copy(3, place(c, 1, x, kind), place(c, 2, x, kind), c, kind, above)

    def other_on(c, kind):
        return kv_copy(4, place(c, 1, 1 - x, kind), place(c, 2, 1 - x, kind), c, kind, above)

    def q_across(c):
        return remote(q_ref.at[:, theirs + c], qq.at[c, x],
                      q_send.at[0, c], q_recv.at[0, c], across)

    def g_across(c):
        return remote(g_ref.at[:, theirs + c], gg.at[c, x],
                      q_send.at[1, c], q_recv.at[1, c], across)

    def far_copy(c, s):
        return remote(far.at[c, s], far_in.at[c, s], far_send.at[c, s], far_recv.at[c, s], below)

    def near_copy(c, s):
        return remote(near.at[c, s], near_in.at[c, s], near_send.at[c, s], near_recv.at[c, s],
                      below)

    last = half - 1

    def near_cross(i, s):
        return remote(near.at[last, s], cross_in.at[i], near_send.at[last, s], cross_recv.at[i],
                      {"ctx": 2 * (p - 1) + 1 - x})

    def part_copy(i):
        return remote(part.at[i], part_in.at[i], part_send.at[i], part_recv.at[i], across)

    def dq_copy(c, i):
        return remote(dq_send.at[c, 2 * (1 - x) + i],
                      dq_ref.at[pl.ds(i * STRIP, STRIP), mine + c],
                      dq_ssem.at[c, i], dq_rsem.at[c, i], across)

    def dq_keep(c, i):
        return pltpu.make_async_copy(dq_send.at[c, 2 * x + i],
                                     dq_ref.at[pl.ds(i * STRIP, STRIP), mine + c],
                                     keep_sem.at[c, i])

    def dkv_copy(c, i, kind):
        return remote(dkv_send.at[c, 2 * (1 - x) + i, kind],
                      (dk_ref, dv_ref)[kind].at[mine + c, pl.ds(i * STRIP, STRIP), :],
                      dkv_ssem.at[c, i, kind], dkv_rsem.at[c, i, kind], across)

    def count_copy(k):
        return remote(count.at[k], count_in.at[k], count_send.at[k], count_recv.at[k],
                      partner(*bits[k]))

    def mark_copy(hop, side):
        k = 2 * hop + side
        return remote(mark_ref, marks.at[2 * hop + x], mark_send.at[k], mark_recv.at[2 * hop + x],
                      {"ctx": 2 * (p + hop) + side})

    def mark_arrival(hop, side):
        k = 2 * hop + side
        return remote(mark_ref, marks.at[k], mark_send.at[k], mark_recv.at[k],
                      {"ctx": 2 * (p + hop) + side})

    raw_copies = [
        pltpu.make_async_copy(ref, raw.at[kind], local_sem.at[kind])
        for kind, ref in enumerate((k_ref, v_ref))
    ]
    own = [
        pltpu.make_async_copy(ref.at[:, mine + c], buffer.at[c, x], own_sem.at[kind, c])
        for c in range(half)
        for kind, (ref, buffer) in enumerate(((q_ref, qq), (g_ref, gg)))
    ]
    for copy in raw_copies:
        copy.start()
    barrier = pltpu.get_barrier_semaphore()

    def greet(device):
        pl.semaphore_signal(barrier, inc=1, device_id=device,
                            device_id_type=pl.DeviceIdType.MESH)

    greet(across)
    for hop in (1, 2):
        for side in (0, 1):
            @pl.when(p + hop < planes)
            def _():
                greet({"ctx": 2 * (p + hop) + side})

            @pl.when(p >= hop)
            def _():
                greet({"ctx": 2 * (p - hop) + side})
    distant = [b for b in bits if b[0] == "dp" or b[1] > 4]
    for b in distant:
        greet(partner(*b))
    for copy in own:
        copy.start()
    for kind, copy in enumerate(raw_copies):
        copy.wait()
        kv_ref[:, kind] = jnp.swapaxes(raw[kind], 0, 1)
    pl.semaphore_wait(
        barrier,
        1 + 2 * jnp.minimum(p, 2) + 2 * jnp.minimum(planes - 1 - p, 2) + len(distant),
    )

    def give(c):
        for kind in (0, 1):
            kv_across(c, kind).start()

    def give_q(c):
        q_across(c).start()
        g_across(c).start()

    def send_own(c):
        @pl.when(up)
        def _():
            for kind in (0, 1):
                own_up(c, kind).start()

    def pass_up(c):
        for kind in (0, 1):
            kv_across(c, kind).wait_recv()

            @pl.when(up)
            def _():
                other_up(c, kind).start()

    def pass_on(copy_in, copy_on, c):
        @pl.when(down)
        def _():
            for kind in (0, 1):
                copy_in(c, kind).wait_recv()

                @pl.when(up)
                def _():
                    copy_on(c, kind).start()

    give(0)
    send_own(0)

    @pl.when(up)
    def _():
        for kind in (0, 1):
            cross_up(0, kind).start()

    line = lax.broadcasted_iota(jnp.int32, mark_ref.shape, 0)
    mark_ref[...] = jnp.where(line == 0, turn_ref[...], mask_ref[...])
    for side in (0, 1):
        @pl.when(x != side)
        def _():
            mark_copy(0, side).start()
    for hop in (1, 2):
        for side in (0, 1):
            @pl.when(p + hop < planes)
            def _():
                mark_copy(hop, side).start()
    ones = jnp.sum(mask_ref[...].astype(jnp.float32), axis=1, keepdims=True)
    count[0] = jnp.broadcast_to(ones, count.shape[1:])
    count_copy(0).start()
    for c in range(1, half):
        give(c)
        give_q(c - 1)
    give_q(half - 1)

    own_place = pltpu.make_async_copy(
        kv_ref.at[pl.ds(mine, half)],
        ext.at[:, :, pl.ds(2 * plane + x * rows, rows), :],
        local_sem.at[2],
    )
    own_place.start()

    for hop in (1, 2):
        @pl.when(p < hop)
        def _():
            def clear(c, carry):
                ext[c, :, (2 - hop) * plane : (3 - hop) * plane, :] = jnp.zeros(
                    (2, plane, ext.shape[3]), ext.dtype
                )
                return carry

            lax.fori_loop(0, half, clear, 0)

    def counted(k):
        count_copy(k).wait_recv()
        count[k + 1] = count[k] + count_in[k]
        if k + 1 < len(bits):
            count_copy(k + 1).start()

    def marks_here(hop):
        for side in (0, 1):
            at = ((2 - hop) * plane + side * rows) // STRIP * STRIP
            k = 2 * hop + side

            def lay(source):
                for part in range(rows // STRIP):
                    line = source[part * STRIP : (part + 1) * STRIP]
                    column[at + part * STRIP : at + (part + 1) * STRIP, :] = jnp.transpose(
                        jnp.broadcast_to(line[None], (STRIP, STRIP))
                    )

            present = (x != side) if hop == 0 else (p >= hop)

            @pl.when(present)
            def _():
                mark_arrival(hop, side).wait_recv()
                lay(marks[k, 0].astype(jnp.float32))

            @pl.when(jnp.logical_not(present))
            def _():
                if hop == 0:
                    marks[k] = mark_ref[...]
                    lay(mark_ref[0].astype(jnp.float32))
                else:
                    column[at : at + rows, :] = jnp.full((rows, STRIP), -1.0, jnp.float32)

    shift = group.bit_length() - 1

    def fill_bias(strip):
        low = strip * STRIP
        lines = marks[low // rows, :, low % rows : low % rows + STRIP]
        wide = (STRIP, STRIP * group)
        spread = (
            lax.broadcasted_iota(jnp.int32, wide, 1) >> shift
        ) == lax.broadcasted_iota(jnp.int32, wide, 0)
        token[strip] = jnp.dot(
            lines.astype(jnp.float32).astype(jnp.bfloat16),
            jnp.where(spread, 1.0, 0.0).astype(jnp.bfloat16),
            preferred_element_type=jnp.float32,
        )
        shape = (SPAN, STRIP * group)
        row = lax.broadcasted_iota(jnp.int32, shape, 1) >> shift
        col = lax.broadcasted_iota(jnp.int32, shape, 0)
        turn = jnp.concatenate([column[low : low + SPAN, :]] * group, axis=1)
        ok = (turn == token[strip, 0:1, :]) & (col > row) & (col <= row + WINDOW)
        bias[strip] = jnp.where(ok, 0.0, MASKED)

    counted(0)
    for hop in (0, 1, 2):
        marks_here(hop)
    pass_on(own_up, own_on, 0)
    counted(1)
    fill_bias(0)
    pass_on(other_up, other_on, 0)
    send_own(1)
    pass_up(1)
    counted(2)
    fill_bias(1)
    fill_bias(2)
    fill_bias(3)
    for kind in (0, 1):
        kv_across(0, kind).wait_recv()
    for k in range(3, len(bits)):
        counted(k)
    for copy in own:
        copy.wait()
    own_place.wait()

    factor = (rows * n * pairs) / count[len(bits), 0:1, 0:1]

    def pass_back(c):
        @pl.when(down)
        def _():
            for s in range(strips):
                at = plane + s * STRIP

                @pl.when(up)
                def _():
                    far_copy(c, s).wait_recv()
                    near[c, s] = (
                        acc[c % 2, :, at : at + STRIP, :] + far_in[c, s].astype(jnp.float32)
                    ).astype(near.dtype)

                @pl.when(jnp.logical_not(up))
                def _():
                    near[c, s] = acc[c % 2, :, at : at + STRIP, :].astype(near.dtype)

                if isinstance(c, int):
                    @pl.when(x == s // 2)
                    def _():
                        near_copy(c, s).start()

                    @pl.when(x != s // 2)
                    def _():
                        near_cross(s % 2, s).start()
                else:
                    near_copy(c, s).start()

    def finish_last():
        slot = last % 2
        for i in range(rows // STRIP):
            at = pl.ds(2 * plane + x * rows + i * STRIP, STRIP)
            own_rows = slice(i * STRIP, (i + 1) * STRIP)

            @pl.when(up)
            def _():
                near_copy(last, 2 * x + i).wait_recv()
                acc[slot, :, at, :] += near_in[last, 2 * x + i].astype(jnp.float32)

            for kind, out in enumerate((dk_ref, dv_ref)):
                scale = factor * SCALE if kind == 0 else factor
                out[mine + last, own_rows, :] = (acc[slot, kind, at, :] * scale).astype(out.dtype)
        for i in range(rows // STRIP):
            own_rows = slice(i * STRIP, (i + 1) * STRIP)
            part_copy(i).wait_recv()

            def deliver(total):
                for kind, out in enumerate((dk_ref, dv_ref)):
                    scale = factor * SCALE if kind == 0 else factor
                    out[theirs + last, own_rows, :] = (total[kind] * scale).astype(out.dtype)

            @pl.when(up)
            def _():
                near_cross(i, 2 * x + i).wait_recv()
                deliver(part_in[i].astype(jnp.float32) + cross_in[i].astype(jnp.float32))

            @pl.when(jnp.logical_not(up))
            def _():
                deliver(part_in[i].astype(jnp.float32))

    def finish(c):
        for s in range(strips):
            side, i = s // 2, s % 2
            at = 2 * plane + s * STRIP

            @pl.when(up)
            def _():
                near_copy(c, s).wait_recv()
                acc[c % 2, :, at : at + STRIP, :] += near_in[c, s].astype(jnp.float32)

            for kind, out in enumerate((dk_ref, dv_ref)):
                scale = factor * SCALE if kind == 0 else factor
                dkv_send[c, s, kind] = (
                    acc[c % 2, kind, at : at + STRIP, :] * scale
                ).astype(dkv_send.dtype)

                @pl.when(x == side)
                def _():
                    out[mine + c, i * STRIP : (i + 1) * STRIP, :] = dkv_send[c, s, kind]

                @pl.when(x != side)
                def _():
                    dkv_copy(c, i, kind).start()

    def step(c, carry):
        @pl.when(c >= 1)
        def _():
            pass_back(c - 1)

        q_across(c).wait_recv()
        g_across(c).wait_recv()

        @pl.when(p >= 2)
        def _():
            for kind in (0, 1):
                own_on(c, kind).wait_recv()
                other_on(c, kind).wait_recv()

        for s in range(strips):
            if s == 3:
                @pl.when(c + 1 < half)
                def _():
                    pass_on(other_up, other_on, c + 1)

                @pl.when(c >= 1)
                def _():
                    finish(c - 1)

            strip_grads(c, s, c % 2, qq, gg, ext, bias, token, acc, factor, dq_send)
            side, i = s // 2, s % 2

            @pl.when(p >= 2)
            def _():
                far[c, s] = acc[c % 2, :, s * STRIP : (s + 1) * STRIP, :].astype(far.dtype)
                far_copy(c, s).start()

            @pl.when(x == side)
            def _():
                dq_keep(c, i).start()

            @pl.when(x != side)
            def _():
                dq_copy(c, i).start()

            if s == 1:
                @pl.when(c + 1 < half)
                def _():
                    pass_on(own_up, own_on, c + 1)

        @pl.when(c + 2 < half)
        def _():
            send_own(c + 2)
            pass_up(c + 2)

        return carry

    lax.fori_loop(0, half, step, 0)
    for i in range(rows // STRIP):
        at = pl.ds(2 * plane + (1 - x) * rows + i * STRIP, STRIP)
        part[i] = acc[last % 2, :, at, :].astype(part.dtype)
        part_copy(i).start()
    pass_back(last)
    finish_last()

    def drain(c, carry):
        q_across(c).wait_send()
        g_across(c).wait_send()
        for i in range(2):
            dq_keep(c, i).wait()
            dq_copy(c, i).wait()

            @pl.when(c < last)
            def _():
                for kind in (0, 1):
                    dkv_copy(c, i, kind).wait()
        for kind in (0, 1):
            kv_across(c, kind).wait_send()

            @pl.when(up)
            def _():
                own_up(c, kind).wait_send()
                other_up(c, kind).wait_send()

                @pl.when(down)
                def _():
                    own_on(c, kind).wait_send()
                    other_on(c, kind).wait_send()

        for s in range(strips):
            @pl.when(down)
            def _():
                near_copy(c, s).wait_send()

            @pl.when(p >= 2)
            def _():
                far_copy(c, s).wait_send()
        return carry

    lax.fori_loop(0, half, drain, 0)
    for i in range(rows // STRIP):
        part_copy(i).wait_send()
    for side in (0, 1):
        @pl.when(x != side)
        def _():
            mark_copy(0, side).wait_send()
    for hop in (1, 2):
        for side in (0, 1):
            @pl.when(p + hop < planes)
            def _():
                mark_copy(hop, side).wait_send()
    for k in range(len(bits)):
        count_copy(k).wait_send()


def place_outputs(dq_in, dk_in, dv_in, dq_out, dk_out, dv_out, held, before, after, sem, out_sem):
    parts = sem.shape[0]
    part = dq_in.shape[0] // parts
    copy = pltpu.make_async_copy
    cuts = [pl.ds(k * part, part) for k in range(parts)]
    loads, stores = [], []
    for n, cut in enumerate(cuts):
        for k, (ref, out) in enumerate(((dk_in, dk_out), (dv_in, dv_out))):
            loads.append(copy(ref.at[:, cut], before.at[k, :, cut], sem.at[n, k]))
            stores.append(copy(after.at[k, cut], out.at[cut], out_sem.at[n, k]))
    whole = [copy(dq_in.at[cut], held.at[cut], sem.at[n, 2]) for n, cut in enumerate(cuts)]
    whole_out = [copy(held.at[cut], dq_out.at[cut], out_sem.at[n, 2]) for n, cut in enumerate(cuts)]
    for load in loads + whole:
        load.start()
    for n in range(parts):
        for k in (0, 1):
            loads[2 * n + k].wait()
            at = slice(n * part, (n + 1) * part)
            after[k, at] = jnp.swapaxes(before[k, :, at], 0, 1)
            stores[2 * n + k].start()
    for load, store in zip(whole, whole_out):
        load.wait()
        store.start()
    for store in stores + whole_out:
        store.wait()


def on_device(queries, keys, values, d_out, loss_mask, turn_ids):
    rows, heads_q, depth = queries.shape[1:]
    heads = keys.shape[2]
    half = heads // 2
    group = heads_q // heads
    n = lax.axis_size("ctx")
    plane = 2 * rows
    strips = rows // STRIP
    wide = group * STRIP
    pairs = lax.axis_size("dp")
    rounds = n.bit_length() + pairs.bit_length() - 2

    def by_group(array):
        return array.reshape(rows, heads, group, depth)

    vmem = pl.BlockSpec(memory_space=pltpu.VMEM)
    anywhere = pl.BlockSpec(memory_space=pl.ANY)
    bf16, f32 = jnp.bfloat16, jnp.float32
    dma = pltpu.SemaphoreType.DMA
    dq, dk, dv = pl.pallas_call(
        functools.partial(kernel, n, pairs, rows),
        out_shape=(
            jax.ShapeDtypeStruct((rows, heads, group, depth), bf16),
            jax.ShapeDtypeStruct((heads, rows, depth), bf16),
            jax.ShapeDtypeStruct((heads, rows, depth), bf16),
        ),
        in_specs=[anywhere] * 4 + [vmem] * 2,
        out_specs=(anywhere, vmem, vmem),
        scratch_shapes=[
            pltpu.VMEM((2, rows, heads, depth), bf16),
            pltpu.VMEM((heads, 2, rows, depth), bf16),
            pltpu.VMEM((half, 2, WINDOW + plane, depth), bf16),
            pltpu.VMEM((half, 2, rows, group, depth), bf16),
            pltpu.VMEM((half, 2, rows, group, depth), bf16),
            pltpu.VMEM((2, 2, WINDOW + plane, depth), f32),
            pltpu.VMEM((2 * strips, SPAN, wide), f32),
            pltpu.VMEM((2 * strips, 8, wide), f32),
            pltpu.VMEM((WINDOW + plane, STRIP), f32),
            pltpu.VMEM((half, 2 * strips, STRIP, group, depth), bf16),
            pltpu.VMEM((half, 2 * strips, 2, STRIP, depth), bf16),
            pltpu.VMEM((half, 2 * strips, 2, STRIP, depth), bf16),
            pltpu.VMEM((half, 2 * strips, 2, STRIP, depth), bf16),
            pltpu.VMEM((half, 2 * strips, 2, STRIP, depth), bf16),
            pltpu.VMEM((half, 2 * strips, 2, STRIP, depth), bf16),
            pltpu.VMEM((strips, 2, STRIP, depth), bf16),
            pltpu.VMEM((strips, 2, STRIP, depth), bf16),
            pltpu.VMEM((strips, 2, STRIP, depth), bf16),
            pltpu.VMEM((8, rows), jnp.int32),
            pltpu.VMEM((6, 8, rows), jnp.int32),
            pltpu.VMEM((rounds + 1, 8, 128), f32),
            pltpu.VMEM((rounds, 8, 128), f32),
            dma((6,)),
            dma((6,)),
            dma((rounds,)),
            dma((rounds,)),
            dma((3,)),
            dma((2, half)),
            dma((half, strips)),
            dma((5, half, 2)),
            dma((5, half, 2)),
            dma((2, half)),
            dma((2, half)),
            dma((half, 2 * strips)),
            dma((half, 2 * strips)),
            dma((half, 2 * strips)),
            dma((half, 2 * strips)),
            dma((half, strips)),
            dma((half, strips)),
            dma((half, strips, 2)),
            dma((half, strips, 2)),
            dma((strips,)),
            dma((strips,)),
            dma((strips,)),
        ],
        compiler_params=pltpu.CompilerParams(
            collective_id=0, has_side_effects=True, vmem_limit_bytes=56 << 20
        ),
    )(by_group(queries[0]), by_group(d_out[0]), keys[0], values[0], turn_ids, loss_mask)
    dq, dk, dv = pl.pallas_call(
        place_outputs,
        out_shape=(
            jax.ShapeDtypeStruct((rows, heads, group, depth), bf16),
            jax.ShapeDtypeStruct((rows, heads, depth), bf16),
            jax.ShapeDtypeStruct((rows, heads, depth), bf16),
        ),
        in_specs=[anywhere] * 3,
        out_specs=(anywhere,) * 3,
        scratch_shapes=[
            pltpu.VMEM((rows, heads, group, depth), bf16),
            pltpu.VMEM((2, heads, rows, depth), bf16),
            pltpu.VMEM((2, rows, heads, depth), bf16),
            dma((2, 3)),
            dma((2, 3)),
        ],
    )(dq, dk, dv)
    return (dq.reshape(1, rows, heads_q, depth), dk[None], dv[None])


def solution(mesh):
    spec = P("dp", "ctx", "head", None)
    return jax.shard_map(
        on_device,
        mesh=mesh,
        in_specs=(spec, spec, spec, spec, P("dp", "ctx"), P("dp", "ctx")),
        out_specs=(spec, spec, spec),
        check_vma=False,
    )
```

```python
import functools
import math

import jax
import jax.numpy as jnp
from jax import lax
from jax.experimental import pallas as pl
from jax.experimental.pallas import tpu as pltpu
from jax.sharding import PartitionSpec as P

WINDOW = 1024
SCALE = 168.0 ** (-0.5)
STRIP = 128
SPAN = WINDOW + STRIP
MASKED = -1e30


def strip_grads(c, strip, slot, qq, gg, ext, bias, token, acc, factor, dq_send):
    low = strip * STRIP
    side, i = low // qq.shape[2], low % qq.shape[2]
    wide = (STRIP * qq.shape[3], qq.shape[4])
    query = qq[c, side, i : i + STRIP].reshape(wide)
    grad = gg[c, side, i : i + STRIP].reshape(wide)
    key = ext[c, 0, low : low + SPAN, :]
    value = ext[c, 1, low : low + SPAN, :]
    logits = lax.dot_general(
        key, query, (((1,), (1,)), ((), ())), preferred_element_type=jnp.float32
    )
    logits = logits * (SCALE * math.log2(math.e)) + bias[strip]
    top = jnp.max(logits, axis=0, keepdims=True)
    raised = jnp.exp2(logits - top)
    prob = raised * (token[strip, 1:2, :] / jnp.sum(raised, axis=0, keepdims=True))
    grad_prob = lax.dot_general(
        value, grad, (((1,), (1,)), ((), ())), preferred_element_type=jnp.float32
    )
    delta = jnp.sum(prob * grad_prob, axis=0, keepdims=True)
    grad_logit = (prob * (grad_prob - delta)).astype(jnp.bfloat16)
    dq = jnp.transpose(
        lax.dot_general(
            key, grad_logit, (((0,), (0,)), ((), ())), preferred_element_type=jnp.float32
        )
    )
    dq = (dq * (factor * SCALE)).astype(jnp.bfloat16)
    dq_send[c, strip] = dq.reshape(dq_send.shape[2:])
    parts = (
        jnp.dot(grad_logit, query, preferred_element_type=jnp.float32),
        jnp.dot(prob.astype(jnp.bfloat16), grad, preferred_element_type=jnp.float32),
    )
    for kind, part in enumerate(parts):
        if strip == 0:
            acc[slot, kind, :SPAN] = part
        else:
            acc[slot, kind, low : low + WINDOW] += part[:WINDOW]
            acc[slot, kind, low + WINDOW : low + SPAN] = part[WINDOW:]


def kernel(
    n, pairs, rows, q_ref, g_ref, k_ref, v_ref, turn_ref, mask_ref,
    dq_ref, dk_ref, dv_ref,
    raw, kv_ref, ext, qq, gg, acc, bias, token, column, dq_send, dkv_send, far, far_in, near, near_in, part, part_in, cross_in,
    mark_ref, marks, count, count_in,
    mark_send, mark_recv, count_send, count_recv, local_sem, own_sem, keep_sem,
    kv_send, kv_recv, q_send, q_recv, far_send, far_recv, near_send, near_recv,
    dq_ssem, dq_rsem, dkv_ssem, dkv_rsem, part_send, part_recv, cross_recv,
):
    heads, group = q_ref.shape[1:3]
    half = heads // 2
    plane = 2 * rows
    planes = n // 2
    strips = plane // STRIP
    me = lax.axis_index("ctx")
    x = me % 2
    p = me // 2
    up, down = p + 1 < planes, p >= 1
    mine, theirs = x * half, (1 - x) * half
    bits = [("ctx", 1 << b) for b in range(n.bit_length() - 1)]
    bits += [("dp", 1 << b) for b in range(pairs.bit_length() - 1)]
    across, above, below = {"ctx": me + 1 - 2 * x}, {"ctx": me + 2}, {"ctx": me - 2}

    def remote(src, dst, send, recv, device):
        return pltpu.make_async_remote_copy(
            src_ref=src, dst_ref=dst, send_sem=send, recv_sem=recv,
            device_id=device, device_id_type=pl.DeviceIdType.MESH,
        )

    def partner(axis, bit):
        at = lax.axis_index(axis)
        return {axis: at + bit - 2 * bit * ((at // bit) % 2)}

    def place(c, hop, side, kind):
        return ext.at[c, kind, pl.ds((2 - hop) * plane + side * rows, rows), :]

    def kv_copy(what, src, dst, c, kind, device):
        return remote(src, dst, kv_send.at[what, c, kind], kv_recv.at[what, c, kind], device)

    def kv_across(c, kind):
        return kv_copy(0, kv_ref.at[theirs + c, kind], place(c, 0, x, kind), c, kind, across)

    def own_up(c, kind):
        return kv_copy(1, kv_ref.at[mine + c, kind], place(c, 1, x, kind), c, kind, above)

    def other_up(c, kind):
        return kv_copy(2, place(c, 0, 1 - x, kind), place(c, 1, 1 - x, kind), c, kind, above)

    def cross_up(c, kind):
        return kv_copy(2, kv_ref.at[theirs + c, kind], place(c, 1, x, kind), c, kind,
                       {"ctx": 2 * (p + 1) + 1 - x})

    def own_on(c, kind):
        return kv_copy(3, place(c, 1, x, kind), place(c, 2, x, kind), c, kind, above)

    def other_on(c, kind):
        return kv_copy(4, place(c, 1, 1 - x, kind), place(c, 2, 1 - x, kind), c, kind, above)

    def q_across(c):
        return remote(q_ref.at[:, theirs + c], qq.at[c, x],
                      q_send.at[0, c], q_recv.at[0, c], across)

    def g_across(c):
        return remote(g_ref.at[:, theirs + c], gg.at[c, x],
                      q_send.at[1, c], q_recv.at[1, c], across)

    def far_copy(c, s):
        return remote(far.at[c, s], far_in.at[c, s], far_send.at[c, s], far_recv.at[c, s], below)

    def near_copy(c, s):
        return remote(near.at[c, s], near_in.at[c, s], near_send.at[c, s], near_recv.at[c, s],
                      below)

    last = half - 1

    def near_cross(i, s):
        return remote(near.at[last, s], cross_in.at[i], near_send.at[last, s], cross_recv.at[i],
                      {"ctx": 2 * (p - 1) + 1 - x})

    def part_copy(i):
        return remote(part.at[i], part_in.at[i], part_send.at[i], part_recv.at[i], across)

    def dq_copy(c, i):
        return remote(dq_send.at[c, 2 * (1 - x) + i],
                      dq_ref.at[pl.ds(i * STRIP, STRIP), mine + c],
                      dq_ssem.at[c, i], dq_rsem.at[c, i], across)

    def dq_keep(c, i):
        return pltpu.make_async_copy(dq_send.at[c, 2 * x + i],
                                     dq_ref.at[pl.ds(i * STRIP, STRIP), mine + c],
                                     keep_sem.at[c, i])

    def dkv_copy(c, i, kind):
        return remote(dkv_send.at[c, 2 * (1 - x) + i, kind],
                      (dk_ref, dv_ref)[kind].at[mine + c, pl.ds(i * STRIP, STRIP), :],
                      dkv_ssem.at[c, i, kind], dkv_rsem.at[c, i, kind], across)

    def count_copy(k):
        return remote(count.at[k], count_in.at[k], count_send.at[k], count_recv.at[k],
                      partner(*bits[k]))

    def mark_copy(hop, side):
        k = 2 * hop + side
        return remote(mark_ref, marks.at[2 * hop + x], mark_send.at[k], mark_recv.at[2 * hop + x],
                      {"ctx": 2 * (p + hop) + side})

    def mark_arrival(hop, side):
        k = 2 * hop + side
        return remote(mark_ref, marks.at[k], mark_send.at[k], mark_recv.at[k],
                      {"ctx": 2 * (p + hop) + side})

    raw_copies = [
        pltpu.make_async_copy(ref, raw.at[kind], local_sem.at[kind])
        for kind, ref in enumerate((k_ref, v_ref))
    ]
    own = [
        pltpu.make_async_copy(ref.at[:, mine + c], buffer.at[c, x], own_sem.at[kind, c])
        for c in range(half)
        for kind, (ref, buffer) in enumerate(((q_ref, qq), (g_ref, gg)))
    ]
    for copy in raw_copies:
        copy.start()
    barrier = pltpu.get_barrier_semaphore()

    def greet(device):
        pl.semaphore_signal(barrier, inc=1, device_id=device,
                            device_id_type=pl.DeviceIdType.MESH)

    greet(across)
    for hop in (1, 2):
        for side in (0, 1):
            @pl.when(p + hop < planes)
            def _():
                greet({"ctx": 2 * (p + hop) + side})

            @pl.when(p >= hop)
            def _():
                greet({"ctx": 2 * (p - hop) + side})
    distant = [b for b in bits if b[0] == "dp" or b[1] > 4]
    for b in distant:
        greet(partner(*b))
    for copy in own:
        copy.start()
    for kind, copy in enumerate(raw_copies):
        copy.wait()
        kv_ref[:, kind] = jnp.swapaxes(raw[kind], 0, 1)
    pl.semaphore_wait(
        barrier,
        1 + 2 * jnp.minimum(p, 2) + 2 * jnp.minimum(planes - 1 - p, 2) + len(distant),
    )

    def give(c):
        for kind in (0, 1):
            kv_across(c, kind).start()

    def give_q(c):
        q_across(c).start()
        g_across(c).start()

    def send_own(c):
        @pl.when(up)
        def _():
            for kind in (0, 1):
                own_up(c, kind).start()

    def pass_up(c):
        for kind in (0, 1):
            kv_across(c, kind).wait_recv()

            @pl.when(up)
            def _():
                other_up(c, kind).start()

    def pass_on(copy_in, copy_on, c):
        @pl.when(down)
        def _():
            for kind in (0, 1):
                copy_in(c, kind).wait_recv()

                @pl.when(up)
                def _():
                    copy_on(c, kind).start()

    give(0)
    send_own(0)

    @pl.when(up)
    def _():
        for kind in (0, 1):
            cross_up(0, kind).start()

    line = lax.broadcasted_iota(jnp.int32, mark_ref.shape, 0)
    mark_ref[...] = jnp.where(line == 0, turn_ref[...], mask_ref[...])
    for side in (0, 1):
        @pl.when(x != side)
        def _():
            mark_copy(0, side).start()
    for hop in (1, 2):
        for side in (0, 1):
            @pl.when(p + hop < planes)
            def _():
                mark_copy(hop, side).start()
    ones = jnp.sum(mask_ref[...].astype(jnp.float32), axis=1, keepdims=True)
    count[0] = jnp.broadcast_to(ones, count.shape[1:])
    count_copy(0).start()
    for c in range(1, half):
        give(c)
        give_q(c - 1)
    give_q(half - 1)

    own_place = pltpu.make_async_copy(
        kv_ref.at[pl.ds(mine, half)],
        ext.at[:, :, pl.ds(2 * plane + x * rows, rows), :],
        local_sem.at[2],
    )
    own_place.start()

    for hop in (1, 2):
        @pl.when(p < hop)
        def _():
            def clear(c, carry):
                ext[c, :, (2 - hop) * plane : (3 - hop) * plane, :] = jnp.zeros(
                    (2, plane, ext.shape[3]), ext.dtype
                )
                return carry

            lax.fori_loop(0, half, clear, 0)

    def counted(k):
        count_copy(k).wait_recv()
        count[k + 1] = count[k] + count_in[k]
        if k + 1 < len(bits):
            count_copy(k + 1).start()

    def marks_here(hop):
        for side in (0, 1):
            at = ((2 - hop) * plane + side * rows) // STRIP * STRIP
            k = 2 * hop + side

            def lay(source):
                for part in range(rows // STRIP):
                    line = source[part * STRIP : (part + 1) * STRIP]
                    column[at + part * STRIP : at + (part + 1) * STRIP, :] = jnp.transpose(
                        jnp.broadcast_to(line[None], (STRIP, STRIP))
                    )

            present = (x != side) if hop == 0 else (p >= hop)

            @pl.when(present)
            def _():
                mark_arrival(hop, side).wait_recv()
                lay(marks[k, 0].astype(jnp.float32))

            @pl.when(jnp.logical_not(present))
            def _():
                if hop == 0:
                    marks[k] = mark_ref[...]
                    lay(mark_ref[0].astype(jnp.float32))
                else:
                    column[at : at + rows, :] = jnp.full((rows, STRIP), -1.0, jnp.float32)

    shift = group.bit_length() - 1

    def fill_bias(strip):
        low = strip * STRIP
        lines = marks[low // rows, :, low % rows : low % rows + STRIP]
        wide = (STRIP, STRIP * group)
        spread = (
            lax.broadcasted_iota(jnp.int32, wide, 1) >> shift
        ) == lax.broadcasted_iota(jnp.int32, wide, 0)
        token[strip] = jnp.dot(
            lines.astype(jnp.float32).astype(jnp.bfloat16),
            jnp.where(spread, 1.0, 0.0).astype(jnp.bfloat16),
            preferred_element_type=jnp.float32,
        )
        shape = (SPAN, STRIP * group)
        row = lax.broadcasted_iota(jnp.int32, shape, 1) >> shift
        col = lax.broadcasted_iota(jnp.int32, shape, 0)
        turn = jnp.concatenate([column[low : low + SPAN, :]] * group, axis=1)
        ok = (turn == token[strip, 0:1, :]) & (col > row) & (col <= row + WINDOW)
        bias[strip] = jnp.where(ok, 0.0, MASKED)

    counted(0)
    for hop in (0, 1, 2):
        marks_here(hop)
    pass_on(own_up, own_on, 0)
    counted(1)
    fill_bias(0)
    pass_on(other_up, other_on, 0)
    send_own(1)
    pass_up(1)
    counted(2)
    fill_bias(1)
    fill_bias(2)
    fill_bias(3)
    for kind in (0, 1):
        kv_across(0, kind).wait_recv()
    for k in range(3, len(bits)):
        counted(k)
    for copy in own:
        copy.wait()
    own_place.wait()

    factor = (rows * n * pairs) / count[len(bits), 0:1, 0:1]

    def pass_back(c):
        @pl.when(down)
        def _():
            for s in range(strips):
                at = plane + s * STRIP

                @pl.when(up)
                def _():
                    far_copy(c, s).wait_recv()
                    near[c, s] = (
                        acc[c % 2, :, at : at + STRIP, :] + far_in[c, s].astype(jnp.float32)
                    ).astype(near.dtype)

                @pl.when(jnp.logical_not(up))
                def _():
                    near[c, s] = acc[c % 2, :, at : at + STRIP, :].astype(near.dtype)

                if isinstance(c, int):
                    @pl.when(x == s // 2)
                    def _():
                        near_copy(c, s).start()

                    @pl.when(x != s // 2)
                    def _():
                        near_cross(s % 2, s).start()
                else:
                    near_copy(c, s).start()

    def finish_last():
        slot = last % 2
        for i in range(rows // STRIP):
            at = pl.ds(2 * plane + x * rows + i * STRIP, STRIP)
            own_rows = slice(i * STRIP, (i + 1) * STRIP)

            @pl.when(up)
            def _():
                near_copy(last, 2 * x + i).wait_recv()
                acc[slot, :, at, :] += near_in[last, 2 * x + i].astype(jnp.float32)

            for kind, out in enumerate((dk_ref, dv_ref)):
                scale = factor * SCALE if kind == 0 else factor
                out[mine + last, own_rows, :] = (acc[slot, kind, at, :] * scale).astype(out.dtype)
        for i in range(rows // STRIP):
            own_rows = slice(i * STRIP, (i + 1) * STRIP)
            part_copy(i).wait_recv()

            def deliver(total):
                for kind, out in enumerate((dk_ref, dv_ref)):
                    scale = factor * SCALE if kind == 0 else factor
                    out[theirs + last, own_rows, :] = (total[kind] * scale).astype(out.dtype)

            @pl.when(up)
            def _():
                near_cross(i, 2 * x + i).wait_recv()
                deliver(part_in[i].astype(jnp.float32) + cross_in[i].astype(jnp.float32))

            @pl.when(jnp.logical_not(up))
            def _():
                deliver(part_in[i].astype(jnp.float32))

    def finish(c):
        for s in range(strips):
            side, i = s // 2, s % 2
            at = 2 * plane + s * STRIP

            @pl.when(up)
            def _():
                near_copy(c, s).wait_recv()
                acc[c % 2, :, at : at + STRIP, :] += near_in[c, s].astype(jnp.float32)

            for kind, out in enumerate((dk_ref, dv_ref)):
                scale = factor * SCALE if kind == 0 else factor
                dkv_send[c, s, kind] = (
                    acc[c % 2, kind, at : at + STRIP, :] * scale
                ).astype(dkv_send.dtype)

                @pl.when(x == side)
                def _():
                    out[mine + c, i * STRIP : (i + 1) * STRIP, :] = dkv_send[c, s, kind]

                @pl.when(x != side)
                def _():
                    dkv_copy(c, i, kind).start()

    def step(c, carry):
        @pl.when(c >= 1)
        def _():
            pass_back(c - 1)

        q_across(c).wait_recv()
        g_across(c).wait_recv()

        @pl.when(p >= 2)
        def _():
            for kind in (0, 1):
                own_on(c, kind).wait_recv()
                other_on(c, kind).wait_recv()

        for s in range(strips):
            if s == 3:
                @pl.when(c + 1 < half)
                def _():
                    pass_on(other_up, other_on, c + 1)

                @pl.when(c + 2 < half)
                def _():
                    send_own(c + 2)
                    pass_up(c + 2)

                @pl.when(c >= 1)
                def _():
                    finish(c - 1)

            strip_grads(c, s, c % 2, qq, gg, ext, bias, token, acc, factor, dq_send)
            side, i = s // 2, s % 2

            @pl.when(p >= 2)
            def _():
                far[c, s] = acc[c % 2, :, s * STRIP : (s + 1) * STRIP, :].astype(far.dtype)
                far_copy(c, s).start()

            @pl.when(x == side)
            def _():
                dq_keep(c, i).start()

            @pl.when(x != side)
            def _():
                dq_copy(c, i).start()

            if s == 1:
                @pl.when(c + 1 < half)
                def _():
                    pass_on(own_up, own_on, c + 1)

        return carry

    lax.fori_loop(0, half, step, 0)
    for i in range(rows // STRIP):
        at = pl.ds(2 * plane + (1 - x) * rows + i * STRIP, STRIP)
        part[i] = acc[last % 2, :, at, :].astype(part.dtype)
        part_copy(i).start()
    pass_back(last)
    finish_last()

    def drain(c, carry):
        q_across(c).wait_send()
        g_across(c).wait_send()
        for i in range(2):
            dq_keep(c, i).wait()
            dq_copy(c, i).wait()

            @pl.when(c < last)
            def _():
                for kind in (0, 1):
                    dkv_copy(c, i, kind).wait()
        for kind in (0, 1):
            kv_across(c, kind).wait_send()

            @pl.when(up)
            def _():
                own_up(c, kind).wait_send()
                other_up(c, kind).wait_send()

                @pl.when(down)
                def _():
                    own_on(c, kind).wait_send()
                    other_on(c, kind).wait_send()

        for s in range(strips):
            @pl.when(down)
            def _():
                near_copy(c, s).wait_send()

            @pl.when(p >= 2)
            def _():
                far_copy(c, s).wait_send()
        return carry

    lax.fori_loop(0, half, drain, 0)
    for i in range(rows // STRIP):
        part_copy(i).wait_send()
    for side in (0, 1):
        @pl.when(x != side)
        def _():
            mark_copy(0, side).wait_send()
    for hop in (1, 2):
        for side in (0, 1):
            @pl.when(p + hop < planes)
            def _():
                mark_copy(hop, side).wait_send()
    for k in range(len(bits)):
        count_copy(k).wait_send()


def place_outputs(dq_in, dk_in, dv_in, dq_out, dk_out, dv_out, held, before, after, sem, out_sem):
    parts = sem.shape[0]
    part = dq_in.shape[0] // parts
    copy = pltpu.make_async_copy
    cuts = [pl.ds(k * part, part) for k in range(parts)]
    loads, stores = [], []
    for n, cut in enumerate(cuts):
        for k, (ref, out) in enumerate(((dk_in, dk_out), (dv_in, dv_out))):
            loads.append(copy(ref.at[:, cut], before.at[k, :, cut], sem.at[n, k]))
            stores.append(copy(after.at[k, cut], out.at[cut], out_sem.at[n, k]))
    whole = [copy(dq_in.at[cut], held.at[cut], sem.at[n, 2]) for n, cut in enumerate(cuts)]
    whole_out = [copy(held.at[cut], dq_out.at[cut], out_sem.at[n, 2]) for n, cut in enumerate(cuts)]
    for load in loads + whole:
        load.start()
    for n in range(parts):
        for k in (0, 1):
            loads[2 * n + k].wait()
            at = slice(n * part, (n + 1) * part)
            after[k, at] = jnp.swapaxes(before[k, :, at], 0, 1)
            stores[2 * n + k].start()
    for load, store in zip(whole, whole_out):
        load.wait()
        store.start()
    for store in stores + whole_out:
        store.wait()


def on_device(queries, keys, values, d_out, loss_mask, turn_ids):
    rows, heads_q, depth = queries.shape[1:]
    heads = keys.shape[2]
    half = heads // 2
    group = heads_q // heads
    n = lax.axis_size("ctx")
    plane = 2 * rows
    strips = rows // STRIP
    wide = group * STRIP
    pairs = lax.axis_size("dp")
    rounds = n.bit_length() + pairs.bit_length() - 2

    def by_group(array):
        return array.reshape(rows, heads, group, depth)

    vmem = pl.BlockSpec(memory_space=pltpu.VMEM)
    anywhere = pl.BlockSpec(memory_space=pl.ANY)
    bf16, f32 = jnp.bfloat16, jnp.float32
    dma = pltpu.SemaphoreType.DMA
    dq, dk, dv = pl.pallas_call(
        functools.partial(kernel, n, pairs, rows),
        out_shape=(
            jax.ShapeDtypeStruct((rows, heads, group, depth), bf16),
            jax.ShapeDtypeStruct((heads, rows, depth), bf16),
            jax.ShapeDtypeStruct((heads, rows, depth), bf16),
        ),
        in_specs=[anywhere] * 4 + [vmem] * 2,
        out_specs=(anywhere, vmem, vmem),
        scratch_shapes=[
            pltpu.VMEM((2, rows, heads, depth), bf16),
            pltpu.VMEM((heads, 2, rows, depth), bf16),
            pltpu.VMEM((half, 2, WINDOW + plane, depth), bf16),
            pltpu.VMEM((half, 2, rows, group, depth), bf16),
            pltpu.VMEM((half, 2, rows, group, depth), bf16),
            pltpu.VMEM((2, 2, WINDOW + plane, depth), f32),
            pltpu.VMEM((2 * strips, SPAN, wide), f32),
            pltpu.VMEM((2 * strips, 8, wide), f32),
            pltpu.VMEM((WINDOW + plane, STRIP), f32),
            pltpu.VMEM((half, 2 * strips, STRIP, group, depth), bf16),
            pltpu.VMEM((half, 2 * strips, 2, STRIP, depth), bf16),
            pltpu.VMEM((half, 2 * strips, 2, STRIP, depth), bf16),
            pltpu.VMEM((half, 2 * strips, 2, STRIP, depth), bf16),
            pltpu.VMEM((half, 2 * strips, 2, STRIP, depth), bf16),
            pltpu.VMEM((half, 2 * strips, 2, STRIP, depth), bf16),
            pltpu.VMEM((strips, 2, STRIP, depth), bf16),
            pltpu.VMEM((strips, 2, STRIP, depth), bf16),
            pltpu.VMEM((strips, 2, STRIP, depth), bf16),
            pltpu.VMEM((8, rows), jnp.int32),
            pltpu.VMEM((6, 8, rows), jnp.int32),
            pltpu.VMEM((rounds + 1, 8, 128), f32),
            pltpu.VMEM((rounds, 8, 128), f32),
            dma((6,)),
            dma((6,)),
            dma((rounds,)),
            dma((rounds,)),
            dma((3,)),
            dma((2, half)),
            dma((half, strips)),
            dma((5, half, 2)),
            dma((5, half, 2)),
            dma((2, half)),
            dma((2, half)),
            dma((half, 2 * strips)),
            dma((half, 2 * strips)),
            dma((half, 2 * strips)),
            dma((half, 2 * strips)),
            dma((half, strips)),
            dma((half, strips)),
            dma((half, strips, 2)),
            dma((half, strips, 2)),
            dma((strips,)),
            dma((strips,)),
            dma((strips,)),
        ],
        compiler_params=pltpu.CompilerParams(
            collective_id=0, has_side_effects=True, vmem_limit_bytes=56 << 20
        ),
    )(by_group(queries[0]), by_group(d_out[0]), keys[0], values[0], turn_ids, loss_mask)
    dq, dk, dv = pl.pallas_call(
        place_outputs,
        out_shape=(
            jax.ShapeDtypeStruct((rows, heads, group, depth), bf16),
            jax.ShapeDtypeStruct((rows, heads, depth), bf16),
            jax.ShapeDtypeStruct((rows, heads, depth), bf16),
        ),
        in_specs=[anywhere] * 3,
        out_specs=(anywhere,) * 3,
        scratch_shapes=[
            pltpu.VMEM((rows, heads, group, depth), bf16),
            pltpu.VMEM((2, heads, rows, depth), bf16),
            pltpu.VMEM((2, rows, heads, depth), bf16),
            dma((2, 3)),
            dma((2, 3)),
        ],
    )(dq, dk, dv)
    return (dq.reshape(1, rows, heads_q, depth), dk[None], dv[None])


def solution(mesh):
    spec = P("dp", "ctx", "head", None)
    return jax.shard_map(
        on_device,
        mesh=mesh,
        in_specs=(spec, spec, spec, spec, P("dp", "ctx"), P("dp", "ctx")),
        out_specs=(spec, spec, spec),
        check_vma=False,
    )
```
